32 devices in a mesh: tok: 8 (over z, x), tp: 4 (over y, core).
Axes of the slice: x: 2, y: 2, z: 4, core: 2. Of those that a mesh axis runs over, the one named last changes fastest.
Arguments:
- resid: bfloat16 [1024, 8192], P('tok', 'tp'), may hold values from -7 to 7
- norm_gain: float32 [8192], P('tp'), may hold values from 0.5 to 1.5
- head_in: bfloat16 [8192, 2048], P('tp'), may hold values from -0.088388348 to 0.088388348
- head_bias: float32 [2048], replicated, may hold values from -3 to 3
- head_out: float32 [16, 128], replicated, may hold values from -0.26516504 to 0.26516504
- targets: float32 [1024, 16], P('tok'), may hold values from -12 to 12
- label_mask: int32 [1024, 16], P('tok'), may hold values 0 or 1
- obj_weight: int32 [16], replicated, may hold values from 1 to 16
Outputs:
- resid_grad: bfloat16 [1024, 8192], P('tok', 'tp')
- gain_grad: float32 [8192], P('tp')
- head_in_grad: float32 [8192, 2048], P('tp', 'tok')
- head_bias_grad: float32 [2048], replicated
The draws below stay inside these ranges and needn't reach their ends.
All inputs are finite; a program needn't handle non-finite values. No bound on the sum of `label_mask` on one device may be relied on, other than what follows from the above.
Results may differ from the reference program's by a relative error of at most 0.0078.
Values may be sent and summed in bfloat16 or wider, within the bound.
No kernel may reach another device: no remote copies, remote signals or barrier semaphores. Data moves between devices by JAX's collectives and lax.ppermute only.
A program may use at most 128 MiB of HBM per device.

```python
import jax
import jax.numpy as jnp
from jax import lax

D = 8192
OBJ = 16
HH = 128
TOKENS = 1024


def shared_direction(key):
    position = jnp.arange(D, dtype=jnp.float32) / (D - 1)
    feature_ramp = 1.0 + 2.0 * position
    sign_flip = jnp.where(jax.random.bernoulli(jax.random.fold_in(key, 101), 0.5, (D,)), 1.0, -1.0)
    leaning = feature_ramp * sign_flip
    return leaning / jnp.sqrt(jnp.sum(leaning * leaning))


def shared_heads(key):
    return jnp.clip(jax.random.normal(jax.random.fold_in(key, 103), (OBJ, HH), jnp.float32), -3.0, 3.0)


def draw_resid(key, part):
    direction = shared_direction(key)
    strength = jax.random.uniform(jax.random.fold_in(key, 105), (TOKENS, 1), jnp.float32, 0.35, 0.55)
    noise_part = jnp.clip(jax.random.normal(jax.random.fold_in(key, 107), (TOKENS, D), jnp.float32), -5.5, 5.5)
    return jnp.clip(noise_part + strength * D ** 0.5 * direction[None, :], -7.0, 7.0).astype(jnp.bfloat16)


def draw_head_in(key, part):
    direction = shared_direction(key)
    head_base = shared_heads(key)
    scale_in = D ** (-0.5)
    noise_part = jnp.clip(jax.random.normal(jax.random.fold_in(key, 109), (D, OBJ * HH), jnp.float32), -6.0, 6.0)
    leaning = 3.2 * scale_in * direction[:, None] * head_base.reshape(1, OBJ * HH)
    return jnp.clip(noise_part * scale_in + leaning, -8.0 * scale_in, 8.0 * scale_in).astype(jnp.bfloat16)


def draw_head_out(key, part):
    return shared_heads(key) * HH ** (-0.5)


def draw_targets(key, part):
    token_ramp = 1.0 + 2.0 * jnp.arange(TOKENS, dtype=jnp.float32)[:, None] / (TOKENS - 1)
    normal_part = jnp.clip(jax.random.normal(jax.random.fold_in(key, 3), (TOKENS, OBJ), jnp.float32), -4.0, 4.0)
    return normal_part * token_ramp


def with_ends(entries, rng, smallest, high):
    shape = entries.shape
    spot = [jax.random.randint(jax.random.fold_in(rng, axis), (), 0, shape[axis]) for axis in range(len(shape))]
    entries = entries.at[tuple(spot)].set(smallest)
    longest = shape.index(max(shape))
    spot[longest] = (spot[longest] + 1) % shape[longest]
    return entries.at[tuple(spot)].set(high)


def centred(stream_key, shape, scale, reach, kind=jnp.bfloat16):
    return jnp.clip(scale * jax.random.normal(stream_key, shape, jnp.float32), -reach, reach).astype(kind)


def setup_inputs(seed: int = 0) -> dict:
    key_list = jax.random.split(jax.random.key(seed), 9)
    return {
        "resid": draw_resid(jax.random.fold_in(key_list[8], 71), 0),
        "norm_gain": jnp.clip(1.0 + 0.1 * jax.random.normal(key_list[1], (D,), jnp.float32), 0.5, 1.5),
        "head_in": draw_head_in(jax.random.fold_in(key_list[8], 71), 0),
        "head_bias": centred(key_list[3], (OBJ * HH,), 0.5, 3.0, jnp.float32),
        "head_out": draw_head_out(jax.random.fold_in(key_list[8], 71), 0),
        "targets": draw_targets(jax.random.fold_in(key_list[8], 71), 0),
        "label_mask": with_ends((jax.random.randint(key_list[6], (TOKENS, OBJ), 0, 2) < 1).astype(jnp.int32), jax.random.fold_in(key_list[6], 1), 0, 1),
        "obj_weight": with_ends(jax.random.randint(key_list[7], (OBJ,), 1, 17), jax.random.fold_in(key_list[7], 1), 1, 16).astype(jnp.int32),
    }


norm_eps = 1e-05
grad_eps = 1e-06
denominator = 8.0

def reference(resid, norm_gain, head_in, head_bias, head_out, targets, label_mask, obj_weight):
    floated = resid.astype(jnp.float32)
    inverse = lax.rsqrt(lax.optimization_barrier(jnp.sum(floated * floated, axis=1, keepdims=True)) / D + norm_eps)
    unit = floated * inverse
    normed = (unit * norm_gain[None, :]).astype(jnp.bfloat16)
    preact = jnp.dot(normed, head_in, preferred_element_type=jnp.float32) + head_bias[None, :]
    count = preact.shape[0]
    cube = preact.reshape(count, OBJ, HH)
    squash = jax.nn.sigmoid(cube)
    scores = lax.optimization_barrier(jnp.sum(cube * squash * head_out[None], axis=2))
    errors = label_mask.astype(jnp.float32) * (scores - targets)
    slopes = squash * (1.0 + cube * (1.0 - squash))
    row_grad = (errors[:, :, None] * head_out[None] * slopes).astype(jnp.bfloat16)
    grad_cube = row_grad.astype(jnp.float32)
    weight_cube = head_in.astype(jnp.float32).reshape(D, OBJ, HH)
    gram = jnp.einsum('doh,dog->ohg', weight_cube, weight_cube, precision=lax.Precision.HIGHEST)
    mapped = jnp.einsum('toh,ohg->tog', grad_cube, gram, precision=lax.Precision.HIGHEST)
    squares = lax.optimization_barrier(jnp.sum(mapped * grad_cube, axis=(0, 2)))
    obj_rms = jnp.sqrt(squares / (TOKENS * D) + grad_eps)
    balance = obj_weight.astype(jnp.float32) / denominator / obj_rms
    balance_cols = jnp.repeat(balance, HH)
    flat_grad = row_grad.reshape(count, OBJ * HH)
    pre_grad = (flat_grad.astype(jnp.float32) * balance_cols[None, :]).astype(jnp.bfloat16)
    norm_grad = jnp.dot(pre_grad, head_in.T, preferred_element_type=jnp.float32)
    weight_sum = jnp.dot(normed.T, flat_grad, preferred_element_type=jnp.float32)
    head_in_grad = weight_sum * balance_cols[None, :] / TOKENS
    head_bias_grad = lax.optimization_barrier(jnp.sum(flat_grad.astype(jnp.float32), axis=0)) * balance_cols / TOKENS
    gain_grad = lax.optimization_barrier(jnp.sum(norm_grad * unit, axis=0)) / TOKENS
    projection = lax.optimization_barrier(jnp.sum(unit * norm_gain[None, :] * norm_grad, axis=1, keepdims=True)) / D
    resid_grad = (inverse * (norm_gain[None, :] * norm_grad - unit * projection)).astype(jnp.bfloat16)
    return (resid_grad, gain_grad, head_in_grad, head_bias_grad)
```

```python
import functools

import jax
import jax.numpy as jnp
from jax import lax
from jax.experimental import pallas as pl
from jax.experimental.pallas import tpu as pltpu
from jax.sharding import PartitionSpec as P

norm_eps = 1e-05
grad_eps = 1e-06
denominator = 8.0
LANES = 128
BF = jnp.bfloat16
F32 = jnp.float32
MIB = 1 << 20


def exchange(value, axis, flip):
    count = lax.axis_size(axis)
    return lax.ppermute(value, axis, [(i, i ^ flip) for i in range(count)])


def params(mib):
    return pltpu.CompilerParams(vmem_limit_bytes=mib * MIB)


def cost(flops, nbytes):
    return pl.CostEstimate(flops=int(flops), bytes_accessed=int(nbytes), transcendentals=0)


def vmem():
    return pl.BlockSpec(memory_space=pltpu.VMEM)


def forward_kernel(core_ref, resid_ref, gain_ref, weight_ref, keep_ref, send_ref, scaled_ref):
    step = pl.program_id(0)
    width = weight_ref.shape[1]
    halves, rows, total = keep_ref.shape
    columns = total - LANES
    core = core_ref[0]

    def put(value, start, size):
        for quarter in range(2 * halves):
            piece = value[quarter * rows : (quarter + 1) * rows]
            half = quarter // 2

            @pl.when(core == quarter % 2)
            def _():
                keep_ref[half, :, pl.ds(start, size)] = piece

            @pl.when(core != quarter % 2)
            def _():
                send_ref[half, :, pl.ds(start, size)] = piece

    @pl.when(step == 0)
    def _():
        floated = resid_ref[...].astype(F32)
        scaled_ref[...] = (floated * gain_ref[...]).astype(BF)
        sums = jnp.sum(floated * floated, axis=1, keepdims=True)
        put(jnp.broadcast_to(sums, (sums.shape[0], LANES)), columns, LANES)

    value = jnp.dot(scaled_ref[...], weight_ref[...], preferred_element_type=F32)
    put(value, pl.multiple_of(step * width, width), width)


def forward(core, resid, gain, weight):
    tokens, features = resid.shape
    columns = weight.shape[1]
    width = 512
    out = jax.ShapeDtypeStruct((2, tokens // 4, columns + LANES), F32)
    whole = pl.BlockSpec(out.shape, lambda i, c: (0, 0, 0))
    return pl.pallas_call(
        forward_kernel,
        out_shape=(out, out),
        grid_spec=pltpu.PrefetchScalarGridSpec(
            num_scalar_prefetch=1,
            grid=(columns // width,),
            in_specs=[
                pl.BlockSpec((tokens, features), lambda i, c: (0, 0)),
                pl.BlockSpec((1, features), lambda i, c: (0, 0)),
                pl.BlockSpec((features, width), lambda i, c: (0, i)),
            ],
            out_specs=(whole, whole),
            scratch_shapes=[pltpu.VMEM((tokens, features), BF)],
        ),
        compiler_params=params(24),
        cost_estimate=cost(2 * tokens * features * columns, 2 * features * columns),
        name="forward",
    )(core, resid, gain, weight)


def merge_kernel(side_ref, keep_ref, recv_ref, mine_ref, send_ref):
    side = side_ref[0]
    mine_ref[...] = keep_ref[side] + recv_ref[side]
    other = keep_ref[1 - side] + recv_ref[1 - side]
    columns = other.shape[1] - LANES
    send_ref[:, :columns] = other[:, :columns].astype(BF)
    tail = other[:, columns:]
    lane = lax.broadcasted_iota(jnp.int32, tail.shape, 1)
    high = tail.astype(BF).astype(F32)
    rest = tail - high
    middle = rest.astype(BF).astype(F32)
    send_ref[:, columns:] = jnp.where(lane == 0, high, jnp.where(lane == 1, middle, rest - middle)).astype(BF)


def merge(side, keep, recv):
    shape = keep.shape[1:]
    return pl.pallas_call(
        merge_kernel,
        out_shape=(jax.ShapeDtypeStruct(shape, F32), jax.ShapeDtypeStruct(shape, BF)),
        in_specs=[pl.BlockSpec(memory_space=pltpu.SMEM), vmem(), vmem()],
        out_specs=(vmem(), vmem()),
        compiler_params=params(8),
        cost_estimate=cost(keep.size, 3 * keep.size),
        name="merge",
    )(side, keep, recv)


def heads_kernel(
    features, me_ref, mine_ref, recv_ref, bias_ref, out_ref, targets_ref, mask_ref, msg_ref, turned_ref
):
    rows = mine_ref.shape[0]
    columns = mine_ref.shape[1] - LANES
    objectives = targets_ref.shape[0]
    hidden = columns // objectives
    start = pl.multiple_of(me_ref[0] * rows, rows)
    turned_ref[0] = targets_ref[...].T
    turned_ref[1] = mask_ref[...].astype(F32).T
    target = turned_ref[0, pl.ds(start, rows), :]
    mask = turned_ref[1, pl.ds(start, rows), :]
    tail = recv_ref[:, columns:].astype(F32)
    sums = mine_ref[:, columns : columns + 1] + ((tail[:, 0:1] + tail[:, 1:2]) + tail[:, 2:3])
    inverse = lax.rsqrt(sums / features + norm_eps)
    lane = lax.broadcasted_iota(jnp.int32, (rows, LANES), 1)
    extra = jnp.zeros((rows, LANES), F32)
    for which in range(objectives):
        cols = slice(which * hidden, (which + 1) * hidden)
        product = (mine_ref[:, cols] + recv_ref[:, cols].astype(F32)) * inverse
        value = product + bias_ref[:, cols]
        squash = jax.nn.sigmoid(value)
        weight = out_ref[:, cols]
        score = jnp.sum(value * squash * weight, axis=1, keepdims=True)
        error = mask[:, which : which + 1] * (score - target[:, which : which + 1])
        grad = (error * weight * (squash * (1.0 + value * (1.0 - squash)))).astype(BF)
        msg_ref[:, cols] = grad
        along = jnp.sum(grad.astype(F32) * product, axis=1, keepdims=True)
        high = along.astype(BF).astype(F32)
        extra = jnp.where(lane == which, high, extra)
        extra = jnp.where(lane == objectives + which, along - high, extra)
    high = inverse.astype(BF).astype(F32)
    rest = inverse - high
    middle = rest.astype(BF).astype(F32)
    extra = jnp.where(lane == 2 * objectives, high, extra)
    extra = jnp.where(lane == 2 * objectives + 1, middle, extra)
    extra = jnp.where(lane == 2 * objectives + 2, rest - middle, extra)
    msg_ref[:, columns:] = extra.astype(BF)


def heads(features, me, mine, recv, bias, head_out, targets, mask):
    tokens = targets.shape[1]
    return pl.pallas_call(
        functools.partial(heads_kernel, features),
        out_shape=jax.ShapeDtypeStruct(mine.shape, BF),
        in_specs=[pl.BlockSpec(memory_space=pltpu.SMEM)] + [vmem()] * 6,
        out_specs=vmem(),
        scratch_shapes=[pltpu.VMEM((2, tokens, targets.shape[0]), F32)],
        compiler_params=params(8),
        cost_estimate=cost(30 * mine.size, 8 * mine.size),
        name="heads",
    )(me, mine, recv, bias, head_out, targets, mask)


def scales(extra, objectives):
    extra = extra.astype(F32)
    at = 2 * objectives
    inverse = (extra[:, at : at + 1] + extra[:, at + 1 : at + 2]) + extra[:, at + 2 : at + 3]
    along = extra[:, :objectives] + extra[:, objectives:at]
    return inverse, along


def gram_kernel(weight_ref, gram_ref):
    step = pl.program_id(0)
    objectives, hidden, _ = gram_ref.shape

    @pl.when(step == 0)
    def _():
        gram_ref[...] = jnp.zeros_like(gram_ref)

    for which in range(objectives):
        block = weight_ref[:, which * hidden : (which + 1) * hidden]
        gram_ref[which] += lax.dot_general(block, block, (((0,), (0,)), ((), ())), preferred_element_type=F32)


def gram_of(weight, objectives, hidden):
    features, columns = weight.shape
    depth = 512
    return pl.pallas_call(
        gram_kernel,
        out_shape=jax.ShapeDtypeStruct((objectives, hidden, hidden), F32),
        grid=(features // depth,),
        in_specs=[pl.BlockSpec((depth, columns), lambda i: (i, 0))],
        out_specs=pl.BlockSpec((objectives, hidden, hidden), lambda i: (0, 0, 0)),
        compiler_params=params(24),
        cost_estimate=cost(2 * features * columns * hidden, 2 * features * columns),
        name="gram",
    )(weight)


def spread_kernel(grad_ref, gram_ref, msg_ref, sums_ref):
    objectives, hidden, _ = gram_ref.shape
    peers, rows, width = msg_ref.shape
    tokens = grad_ref.shape[0]
    columns = objectives * hidden
    inverse, _ = scales(grad_ref[:, columns:], objectives)
    lane = lax.broadcasted_iota(jnp.int32, (1, width), 1)
    squares = jnp.zeros((1, width), F32)
    for which in range(objectives):
        block = grad_ref[:, which * hidden : (which + 1) * hidden]
        pair = lax.dot_general(block, block, (((0,), (0,)), ((), ())), preferred_element_type=F32)
        total = jnp.sum(jnp.sum(pair * gram_ref[which], axis=0, keepdims=True), axis=1, keepdims=True)
        squares = jnp.where(lane == which, total, squares)
    for peer in range(peers):
        piece = grad_ref[:, peer * width : (peer + 1) * width].astype(F32)
        sums_ref[:, peer * width : (peer + 1) * width] = jnp.sum(piece, axis=0, keepdims=True)
        msg_ref[peer, :tokens, :] = (piece * inverse).astype(BF)
    high = squares.astype(BF).astype(F32)
    rest = squares - high
    middle = rest.astype(BF).astype(F32)
    row = lax.broadcasted_iota(jnp.int32, (rows - tokens, width), 0)
    tail = jnp.where(row == 0, high, jnp.where(row == 1, middle, jnp.where(row == 2, rest - middle, 0.0)))
    for peer in range(peers):
        msg_ref[peer, tokens:, :] = tail.astype(BF)


def spread(grad, gram, peers):
    tokens = grad.shape[0]
    columns = gram.shape[0] * gram.shape[1]
    return pl.pallas_call(
        spread_kernel,
        out_shape=(
            jax.ShapeDtypeStruct((peers, tokens + 16, columns // peers), BF),
            jax.ShapeDtypeStruct((1, columns), F32),
        ),
        in_specs=[vmem(), vmem()],
        out_specs=(vmem(), vmem()),
        compiler_params=params(16),
        cost_estimate=cost(2 * tokens * columns * gram.shape[1], 8 * grad.size),
        name="spread",
    )(grad, gram)


def backward_kernel(
    total, resid_ref, gain_ref, weight_ref, grad_ref, bal_ref, share_ref, out_ref, sum_ref, pre_ref, scal_ref
):
    columns = weight_ref.shape[1]
    objectives = share_ref.shape[1]

    @pl.when(pl.program_id(0) == 0)
    def _():
        pre_ref[...] = (grad_ref[:, :columns].astype(F32) * bal_ref[...]).astype(BF)
        inverse, along = scales(grad_ref[:, columns:], objectives)
        projection = jnp.sum(along * share_ref[...], axis=1, keepdims=True) / total
        scal_ref[0] = jnp.broadcast_to(inverse, scal_ref.shape[1:])
        scal_ref[1] = jnp.broadcast_to(projection, scal_ref.shape[1:])

    grad = lax.dot_general(pre_ref[...], weight_ref[...], (((1,), (1,)), ((), ())), preferred_element_type=F32)
    inverse = scal_ref[0, :, 0:1]
    unit = resid_ref[...].astype(F32) * inverse
    sum_ref[...] = jnp.sum(grad * unit, axis=0, keepdims=True)
    out_ref[...] = (inverse * (gain_ref[...] * grad - unit * scal_ref[1, :, 0:1])).astype(BF)


def backward(total, resid, gain, weight, grad, bal_cols, balance):
    tokens, features = resid.shape
    columns = weight.shape[1]
    depth = 256
    return pl.pallas_call(
        functools.partial(backward_kernel, total),
        out_shape=(jax.ShapeDtypeStruct(resid.shape, BF), jax.ShapeDtypeStruct((1, features), F32)),
        grid=(features // depth,),
        in_specs=[
            pl.BlockSpec((tokens, depth), lambda i: (0, i)),
            pl.BlockSpec((1, depth), lambda i: (0, i)),
            pl.BlockSpec((depth, columns), lambda i: (i, 0)),
            pl.BlockSpec(grad.shape, lambda i: (0, 0)),
            pl.BlockSpec(bal_cols.shape, lambda i: (0, 0)),
            pl.BlockSpec(balance.shape, lambda i: (0, 0)),
        ],
        out_specs=(
            pl.BlockSpec((tokens, depth), lambda i: (0, i)),
            pl.BlockSpec((1, depth), lambda i: (0, i)),
        ),
        scratch_shapes=[pltpu.VMEM((tokens, columns), BF), pltpu.VMEM((2, tokens, LANES), F32)],
        compiler_params=params(24),
        cost_estimate=cost(2 * tokens * features * columns, 2 * features * columns),
        name="backward",
    )(resid, gain, weight, grad, bal_cols, balance)


def weight_kernel(me_ref, gain_ref, scale_ref, grad_ref, *rest):
    block_refs, out_ref, turned_ref = rest[:-2], rest[-2], rest[-1]
    tokens = block_refs[0].shape[0]

    @pl.when(pl.program_id(0) == 0)
    def _():
        for flip in range(len(block_refs)):
            piece = grad_ref[me_ref[0] ^ flip, :tokens, :]
            turned_ref[:, flip * tokens : (flip + 1) * tokens] = piece.T

    blocks = jnp.concatenate([ref[...] for ref in block_refs], axis=0)
    value = jnp.dot(turned_ref[...], blocks, preferred_element_type=F32)
    out_ref[...] = (value * gain_ref[...]).T * scale_ref[...]


def weight_grad(me, gain, col_scale, grads, blocks):
    tokens, features = blocks[0].shape
    columns = grads.shape[2]
    depth = 256
    return pl.pallas_call(
        weight_kernel,
        out_shape=jax.ShapeDtypeStruct((features, columns), F32),
        grid_spec=pltpu.PrefetchScalarGridSpec(
            num_scalar_prefetch=1,
            grid=(features // depth,),
            in_specs=[
                pl.BlockSpec((1, depth), lambda i, m: (0, i)),
                pl.BlockSpec(col_scale.shape, lambda i, m: (0, 0)),
                pl.BlockSpec(grads.shape, lambda i, m: (0, 0, 0)),
            ]
            + [pl.BlockSpec((tokens, depth), lambda i, m: (0, i))] * len(blocks),
            out_specs=pl.BlockSpec((depth, columns), lambda i, m: (i, 0)),
            scratch_shapes=[pltpu.VMEM((columns, tokens * len(blocks)), BF)],
        ),
        compiler_params=params(24),
        cost_estimate=cost(2 * tokens * len(blocks) * features * columns, 8 * features * columns),
        name="weights",
    )(me, gain, col_scale, grads, *blocks)


def gather_blocks(resid):
    count = lax.axis_size("tok")
    found = {0: resid}
    for flip in range(2, count, 2):
        found[flip] = exchange(resid, "tok", flip)
    for flip in range(0, count, 2):
        found[flip + 1] = exchange(found[flip], "tok", 1)
    return [found[flip] for flip in range(count)]


def fast_device(resid, norm_gain, head_in, head_bias, head_out, targets, label_mask, obj_weight):
    tokens, features = resid.shape
    objectives, hidden = head_out.shape
    columns = objectives * hidden
    peers = lax.axis_size("tok")
    total_features = features * lax.axis_size("tp")
    total_tokens = tokens * peers
    me = lax.axis_index("tp")
    place = lax.axis_index("tok")
    gain = norm_gain[None, :]

    keep, send = forward((me % 2)[None], resid, gain, head_in)
    blocks = gather_blocks(resid)
    recv = exchange(send, "tp", 1)
    mine, send = merge((me // 2)[None], keep, recv)
    recv = exchange(send, "tp", 2)
    gram = gram_of(head_in, objectives, hidden)
    part = heads(
        total_features,
        me[None],
        mine,
        recv,
        head_bias[None, :],
        head_out.reshape(1, columns),
        targets.T,
        label_mask.T,
    )
    grad = lax.all_gather(part, "tp", axis=0, tiled=True)
    message, col_sums = spread(grad, gram, peers)
    grads = lax.all_to_all(message, "tok", 0, 0)
    squares = jnp.sum(grads[:, tokens : tokens + 3, :objectives].astype(F32), axis=(0, 1))
    squares = lax.psum(squares, "tp")
    obj_rms = jnp.sqrt(squares / (total_tokens * total_features) + grad_eps)
    balance = obj_weight.astype(F32) / denominator / obj_rms
    bal_cols = jnp.repeat(balance, hidden)
    resid_grad, gain_part = backward(
        total_features, resid, gain, head_in, grad, bal_cols[None, :], balance[None, :]
    )
    sums = lax.psum(jnp.concatenate([gain_part, col_sums], axis=0), "tok")
    gain_grad = sums[0] / total_tokens
    head_bias_grad = sums[1] * bal_cols / total_tokens
    width = columns // peers
    col_scale = lax.dynamic_slice_in_dim(bal_cols, place * width, width, 0) / total_tokens
    head_in_grad = weight_grad(place[None], gain, col_scale[None, :], grads, blocks)
    return (resid_grad, gain_grad, head_in_grad, head_bias_grad)


def head_gradient(preact, head_out, targets, label_mask):
    count = preact.shape[0]
    objectives, hidden = head_out.shape
    cube = preact.reshape(count, objectives, hidden)
    squash = jax.nn.sigmoid(cube)
    scores = jnp.sum(cube * squash * head_out[None], axis=2)
    errors = label_mask.astype(jnp.float32) * (scores - targets)
    slopes = squash * (1.0 + cube * (1.0 - squash))
    row_grad = (errors[:, :, None] * head_out[None] * slopes).astype(jnp.bfloat16)
    return row_grad.reshape(count, objectives * hidden)


def general_device(resid, norm_gain, head_in, head_bias, head_out, targets, label_mask, obj_weight):
    tok_rows = resid.shape[0]
    total_features = resid.shape[1] * lax.axis_size("tp")
    objectives, hidden = head_out.shape
    total_tokens = tok_rows * lax.axis_size("tok")
    floated = resid.astype(jnp.float32)
    row_sums = lax.psum(jnp.sum(floated * floated, axis=1), "tp")
    inverse = lax.rsqrt(row_sums[:, None] / total_features + norm_eps)
    unit = floated * inverse
    normed = (unit * norm_gain[None, :]).astype(jnp.bfloat16)
    partial_value = jnp.dot(normed, head_in, preferred_element_type=jnp.float32)
    quarter = lax.psum_scatter(partial_value, "tp", scatter_dimension=0, tiled=True)
    share = quarter.shape[0]
    offset = lax.axis_index("tp") * share
    part_targets = lax.dynamic_slice_in_dim(targets, offset, share, 0)
    part_mask = lax.dynamic_slice_in_dim(label_mask, offset, share, 0)
    part_grad = head_gradient(quarter + head_bias[None, :], head_out, part_targets, part_mask)
    row_grad = lax.all_gather(part_grad, "tp", axis=0, tiled=True)
    grad_float = row_grad.astype(jnp.float32)

    def objective_square(which):
        grad_slice = lax.dynamic_slice_in_dim(row_grad, which * hidden, hidden, 1)
        weight_slice = lax.dynamic_slice_in_dim(head_in, which * hidden, hidden, 1)
        feature_grad = lax.dot_general(
            grad_slice, weight_slice, (((1,), (1,)), ((), ())), preferred_element_type=jnp.float32
        )
        return jnp.sum(feature_grad * feature_grad)

    local_squares = lax.map(objective_square, jnp.arange(objectives))
    squares = lax.psum(local_squares, ("tok", "tp"))
    obj_rms = jnp.sqrt(squares / (total_tokens * total_features) + grad_eps)
    balance = obj_weight.astype(jnp.float32) / denominator / obj_rms
    balance_cols = jnp.repeat(balance, hidden)
    pre_grad = (grad_float * balance_cols[None, :]).astype(jnp.bfloat16)
    norm_grad = lax.dot_general(
        pre_grad, head_in, (((1,), (1,)), ((), ())), preferred_element_type=jnp.float32
    )
    gain_sum, bias_sum = lax.psum(
        (jnp.sum(norm_grad * unit, axis=0), jnp.sum(grad_float, axis=0)), "tok"
    )
    gain_grad = gain_sum / total_tokens
    head_bias_grad = bias_sum * balance_cols / total_tokens
    projection = lax.psum(jnp.sum(unit * norm_gain[None, :] * norm_grad, axis=1), "tp")
    resid_grad = (
        inverse * (norm_gain[None, :] * norm_grad - unit * (projection[:, None] / total_features))
    ).astype(jnp.bfloat16)
    weight_term = lax.dot_general(
        normed, row_grad, (((0,), (0,)), ((), ())), preferred_element_type=jnp.float32
    )
    summed_block = lax.psum_scatter(weight_term, "tok", scatter_dimension=1, tiled=True)
    columns = summed_block.shape[1]
    col_scale = lax.dynamic_slice_in_dim(balance_cols, lax.axis_index("tok") * columns, columns, 0)
    head_in_grad = summed_block * col_scale[None, :] / total_tokens
    return (resid_grad, gain_grad, head_in_grad, head_bias_grad)


def per_device(mesh, *args):
    resid, _, head_in, _, head_out = args[:5]
    peers, shards = mesh.shape["tok"], mesh.shape["tp"]
    columns = head_in.shape[1]
    width = columns // peers
    fits = shards == 4 and peers & (peers - 1) == 0 and columns % peers == 0
    fits = fits and width % LANES == 0 and head_out.shape[1] == LANES and head_out.shape[0] <= 32
    fits = fits and resid.shape[0] % 128 == 0 and resid.shape[1] % 512 == 0 and columns % 512 == 0
    return (fast_device if fits else general_device)(*args)


def solution(mesh):
    return jax.shard_map(
        functools.partial(per_device, mesh),
        mesh=mesh,
        in_specs=(
            P("tok", "tp"),
            P("tp"),
            P("tp", None),
            P(),
            P(),
            P("tok", None),
            P("tok", None),
            P(),
        ),
        out_specs=(P("tok", "tp"), P("tp"), P("tp", "tok"), P()),
        check_vma=False,
    )
```

```python
import functools

import jax
import jax.numpy as jnp
from jax import lax
from jax.experimental import pallas as pl
from jax.experimental.pallas import tpu as pltpu
from jax.sharding import PartitionSpec as P


norm_eps = 1e-05
grad_eps = 1e-06
denominator = 8.0
LANES = 128
BF = jnp.bfloat16
F32 = jnp.float32
MIB = 1 << 20
BIG = 57


def exchange(value, axis, flip):
    count = lax.axis_size(axis)
    return lax.ppermute(value, axis, [(i, i ^ flip) for i in range(count)])


def params(mib):
    return pltpu.CompilerParams(vmem_limit_bytes=mib * MIB)


def cost(flops, nbytes):
    return pl.CostEstimate(flops=int(flops), bytes_accessed=int(nbytes), transcendentals=0)


def vmem():
    return pl.BlockSpec(memory_space=pltpu.VMEM)


def fetch_columns(source, target, sems):
    width = target.shape[1] // sems.shape[0]

    def copy(i):
        part = pl.ds(pl.multiple_of(i * width, width), width)
        return pltpu.make_async_copy(source.at[:, part], target.at[:, part], sems.at[i])

    for i in range(sems.shape[0]):
        copy(i).start()
    return copy, width


def fetch_rows(source, target, sems):
    depth = target.shape[0] // sems.shape[0]

    def copy(i):
        part = pl.ds(pl.multiple_of(i * depth, depth), depth)
        return pltpu.make_async_copy(source.at[part, :], target.at[part, :], sems.at[i])

    for i in range(sems.shape[0]):
        copy(i).start()
    return copy, depth


def smem():
    return pl.BlockSpec(memory_space=pltpu.SMEM)


def hbm():
    return pl.BlockSpec(memory_space=pl.ANY)


def forward_kernel(core_ref, resid_ref, gain_ref, weight_hbm, keep_ref, send_ref, weight_ref, scaled_ref, sems):
    halves, rows, total = keep_ref.shape
    columns = total - LANES
    core = core_ref[0]
    copy, width = fetch_columns(weight_hbm, weight_ref, sems)

    def put(value, cols):
        for quarter in range(2 * halves):
            piece = value[quarter * rows : (quarter + 1) * rows]
            half = quarter // 2

            @pl.when(core == quarter % 2)
            def _():
                keep_ref[half, :, cols] = piece

            @pl.when(core != quarter % 2)
            def _():
                send_ref[half, :, cols] = piece

    floated = resid_ref[...].astype(F32)
    scaled_ref[...] = (floated * gain_ref[...]).astype(BF)
    sums = jnp.sum(floated * floated, axis=1, keepdims=True)
    put(jnp.broadcast_to(sums, (sums.shape[0], LANES)), pl.ds(columns, LANES))

    @pl.loop(0, sems.shape[0])
    def _(i):
        copy(i).wait()
        cols = pl.ds(pl.multiple_of(i * width, width), width)
        put(jnp.dot(scaled_ref[...], weight_ref[:, cols], preferred_element_type=F32), cols)


def forward(core, resid, gain, weight):
    tokens, features = resid.shape
    columns = weight.shape[1]
    out = jax.ShapeDtypeStruct((2, tokens // 4, columns + LANES), F32)
    return pl.pallas_call(
        forward_kernel,
        out_shape=(out, out),
        in_specs=[smem(), vmem(), vmem(), hbm()],
        out_specs=(vmem(), vmem()),
        scratch_shapes=[
            pltpu.VMEM(weight.shape, BF),
            pltpu.VMEM((tokens, features), BF),
            pltpu.SemaphoreType.DMA((4,)),
        ],
        compiler_params=params(BIG),
        cost_estimate=cost(2 * tokens * features * columns, 2 * features * columns),
        name="forward",
    )(core, resid, gain, weight)


def merge_kernel(side_ref, keep_ref, recv_ref, mine_ref, send_ref):
    side = side_ref[0]
    mine_ref[...] = keep_ref[side] + recv_ref[side]
    other = keep_ref[1 - side] + recv_ref[1 - side]
    columns = other.shape[1] - LANES
    send_ref[:, :columns] = other[:, :columns].astype(BF)
    tail = other[:, columns:]
    lane = lax.broadcasted_iota(jnp.int32, tail.shape, 1)
    high = tail.astype(BF).astype(F32)
    rest = tail - high
    middle = rest.astype(BF).astype(F32)
    send_ref[:, columns:] = jnp.where(lane == 0, high, jnp.where(lane == 1, middle, rest - middle)).astype(BF)


def merge(side, keep, recv):
    shape = keep.shape[1:]
    return pl.pallas_call(
        merge_kernel,
        out_shape=(jax.ShapeDtypeStruct(shape, F32), jax.ShapeDtypeStruct(shape, BF)),
        in_specs=[pl.BlockSpec(memory_space=pltpu.SMEM), vmem(), vmem()],
        out_specs=(vmem(), vmem()),
        compiler_params=params(8),
        cost_estimate=cost(keep.size, 3 * keep.size),
        name="merge",
    )(side, keep, recv)


def heads_kernel(
    features, me_ref, mine_ref, recv_ref, bias_ref, out_ref, targets_ref, mask_ref, msg_ref, turned_ref
):
    rows = mine_ref.shape[0]
    columns = mine_ref.shape[1] - LANES
    objectives = targets_ref.shape[0]
    hidden = columns // objectives
    start = pl.multiple_of(me_ref[0] * rows, rows)
    turned_ref[0] = targets_ref[...].T
    turned_ref[1] = mask_ref[...].astype(F32).T
    target = turned_ref[0, pl.ds(start, rows), :]
    mask = turned_ref[1, pl.ds(start, rows), :]
    tail = recv_ref[:, columns:].astype(F32)
    sums = mine_ref[:, columns : columns + 1] + ((tail[:, 0:1] + tail[:, 1:2]) + tail[:, 2:3])
    inverse = lax.rsqrt(sums / features + norm_eps)
    lane = lax.broadcasted_iota(jnp.int32, (rows, LANES), 1)
    extra = jnp.zeros((rows, LANES), F32)
    for which in range(objectives):
        cols = slice(which * hidden, (which + 1) * hidden)
        product = (mine_ref[:, cols] + recv_ref[:, cols].astype(F32)) * inverse
        value = product + bias_ref[:, cols]
        squash = jax.nn.sigmoid(value)
        weight = out_ref[:, cols]
        score = jnp.sum(value * squash * weight, axis=1, keepdims=True)
        error = mask[:, which : which + 1] * (score - target[:, which : which + 1])
        grad = (error * weight * (squash * (1.0 + value * (1.0 - squash)))).astype(BF)
        msg_ref[:, cols] = grad
        along = jnp.sum(grad.astype(F32) * product, axis=1, keepdims=True)
        high = along.astype(BF).astype(F32)
        extra = jnp.where(lane == which, high, extra)
        extra = jnp.where(lane == objectives + which, along - high, extra)
    high = inverse.astype(BF).astype(F32)
    rest = inverse - high
    middle = rest.astype(BF).astype(F32)
    extra = jnp.where(lane == 2 * objectives, high, extra)
    extra = jnp.where(lane == 2 * objectives + 1, middle, extra)
    extra = jnp.where(lane == 2 * objectives + 2, rest - middle, extra)
    msg_ref[:, columns:] = extra.astype(BF)


def heads(features, me, mine, recv, bias, head_out, targets, mask):
    tokens = targets.shape[1]
    return pl.pallas_call(
        functools.partial(heads_kernel, features),
        out_shape=jax.ShapeDtypeStruct(mine.shape, BF),
        in_specs=[pl.BlockSpec(memory_space=pltpu.SMEM)] + [vmem()] * 6,
        out_specs=vmem(),
        scratch_shapes=[pltpu.VMEM((2, tokens, targets.shape[0]), F32)],
        compiler_params=params(8),
        cost_estimate=cost(30 * mine.size, 8 * mine.size),
        name="heads",
    )(me, mine, recv, bias, head_out, targets, mask)


def scales(extra, objectives):
    extra = extra.astype(F32)
    at = 2 * objectives
    inverse = (extra[:, at : at + 1] + extra[:, at + 1 : at + 2]) + extra[:, at + 2 : at + 3]
    along = extra[:, :objectives] + extra[:, objectives:at]
    return inverse, along


def gram_kernel(weight_hbm, gram_ref, weight_ref, sems):
    objectives, hidden, _ = gram_ref.shape
    copy, width = fetch_columns(weight_hbm, weight_ref, sems)
    for which in range(objectives):
        if which * hidden % width == 0:
            copy(which * hidden // width).wait()
        block = weight_ref[:, which * hidden : (which + 1) * hidden]
        gram_ref[which] = lax.dot_general(block, block, (((0,), (0,)), ((), ())), preferred_element_type=F32)


def gram_of(weight, objectives, hidden):
    features, columns = weight.shape
    return pl.pallas_call(
        gram_kernel,
        out_shape=jax.ShapeDtypeStruct((objectives, hidden, hidden), F32),
        in_specs=[hbm()],
        out_specs=vmem(),
        scratch_shapes=[pltpu.VMEM(weight.shape, BF), pltpu.SemaphoreType.DMA((4,))],
        compiler_params=params(BIG),
        cost_estimate=cost(2 * features * columns * hidden, 2 * features * columns),
        name="gram",
    )(weight)


def spread_kernel(spot_ref, part0_ref, part1_ref, part2_ref, part3_ref, gram_ref, grad_ref, msg_ref, sums_ref):
    objectives, hidden, _ = gram_ref.shape
    peers, rows, width = msg_ref.shape
    tokens = grad_ref.shape[0]
    columns = objectives * hidden
    share = tokens // 4
    for flip, part_ref in enumerate((part0_ref, part1_ref, part2_ref, part3_ref)):
        start = pl.multiple_of((spot_ref[0] ^ flip) * share, share)
        grad_ref[pl.ds(start, share), :] = part_ref[...]
    inverse, _ = scales(grad_ref[:, columns:], objectives)
    lane = lax.broadcasted_iota(jnp.int32, (1, width), 1)
    squares = jnp.zeros((1, width), F32)
    for which in range(objectives):
        block = grad_ref[:, which * hidden : (which + 1) * hidden]
        pair = lax.dot_general(block, block, (((0,), (0,)), ((), ())), preferred_element_type=F32)
        total = jnp.sum(jnp.sum(pair * gram_ref[which], axis=0, keepdims=True), axis=1, keepdims=True)
        squares = jnp.where(lane == which, total, squares)
    for peer in range(peers):
        piece = grad_ref[:, peer * width : (peer + 1) * width].astype(F32)
        sums_ref[:, peer * width : (peer + 1) * width] = jnp.sum(piece, axis=0, keepdims=True)
        msg_ref[peer, :tokens, :] = (piece * inverse).astype(BF)
    high = squares.astype(BF).astype(F32)
    rest = squares - high
    middle = rest.astype(BF).astype(F32)
    row = lax.broadcasted_iota(jnp.int32, (rows - tokens, width), 0)
    tail = jnp.where(row == 0, high, jnp.where(row == 1, middle, jnp.where(row == 2, rest - middle, 0.0)))
    for peer in range(peers):
        msg_ref[peer, tokens:, :] = tail.astype(BF)


def spread(me, parts, gram, peers):
    share, total = parts[0].shape
    tokens = 4 * share
    columns = gram.shape[0] * gram.shape[1]
    return pl.pallas_call(
        spread_kernel,
        out_shape=(
            jax.ShapeDtypeStruct((tokens, total), BF),
            jax.ShapeDtypeStruct((peers, tokens + 16, columns // peers), BF),
            jax.ShapeDtypeStruct((1, columns), F32),
        ),
        in_specs=[pl.BlockSpec(memory_space=pltpu.SMEM)] + [vmem()] * 5,
        out_specs=(vmem(), vmem(), vmem()),
        compiler_params=params(16),
        cost_estimate=cost(2 * tokens * columns * gram.shape[1], 8 * tokens * total),
        name="spread",
    )(me, *parts, gram)


def products_kernel(resid_ref, weight_hbm, grad_ref, along_ref, weight_ref, scal_ref, sems):
    objectives = along_ref.shape[0]
    columns = weight_hbm.shape[1]
    hidden = columns // objectives
    copy, depth = fetch_rows(weight_hbm, weight_ref, sems)
    inverse, _ = scales(grad_ref[:, columns:], objectives)
    scal_ref[...] = jnp.broadcast_to(inverse, scal_ref.shape)

    @pl.loop(0, sems.shape[0])
    def _(i):
        copy(i).wait()
        rows = pl.ds(pl.multiple_of(i * depth, depth), depth)
        unit = resid_ref[:, rows].astype(F32) * scal_ref[:, 0:1]
        for which in range(objectives):
            cols = slice(which * hidden, (which + 1) * hidden)
            value = lax.dot_general(
                grad_ref[:, cols], weight_ref[rows, cols], (((1,), (1,)), ((), ())), preferred_element_type=F32
            )
            along_ref[which : which + 1, rows] = jnp.sum(value * unit, axis=0, keepdims=True)


def products(resid, weight, grad, objectives):
    tokens, features = resid.shape
    return pl.pallas_call(
        products_kernel,
        out_shape=jax.ShapeDtypeStruct((objectives, features), F32),
        in_specs=[vmem(), hbm(), vmem()],
        out_specs=vmem(),
        scratch_shapes=[
            pltpu.VMEM(weight.shape, BF),
            pltpu.VMEM((tokens, LANES), F32),
            pltpu.SemaphoreType.DMA((4,)),
        ],
        compiler_params=params(BIG),
        cost_estimate=cost(2 * weight.size * tokens, 2 * weight.size),
        name="products",
    )(resid, weight, grad)


def backward_kernel(
    total, bal_ref, share_ref, resid_ref, gain_ref, weight_hbm, grad_ref, out_ref, weight_ref, pre_ref, scal_ref, sems
):
    columns = weight_hbm.shape[1]
    copy, depth = fetch_rows(weight_hbm, weight_ref, sems)
    pre_ref[...] = (grad_ref[:, :columns].astype(F32) * bal_ref[...]).astype(BF)
    inverse, along = scales(grad_ref[:, columns:], share_ref.shape[1])
    scal_ref[0] = jnp.broadcast_to(inverse, scal_ref.shape[1:])
    projection = jnp.sum(along * share_ref[...], axis=1, keepdims=True) / total
    scal_ref[1] = jnp.broadcast_to(projection, scal_ref.shape[1:])

    @pl.loop(0, sems.shape[0])
    def _(i):
        copy(i).wait()
        rows = pl.ds(pl.multiple_of(i * depth, depth), depth)
        grad = lax.dot_general(
            pre_ref[...], weight_ref[rows, :], (((1,), (1,)), ((), ())), preferred_element_type=F32
        )
        inverse = scal_ref[0, :, 0:1]
        unit = resid_ref[:, rows].astype(F32) * inverse
        out_ref[:, rows] = (inverse * (gain_ref[:, rows] * grad - unit * scal_ref[1, :, 0:1])).astype(BF)


def backward(total, resid, gain, weight, grad, bal_cols, balance):
    tokens, _ = resid.shape
    return pl.pallas_call(
        functools.partial(backward_kernel, total),
        out_shape=jax.ShapeDtypeStruct(resid.shape, BF),
        in_specs=[vmem(), vmem(), vmem(), vmem(), hbm(), vmem()],
        out_specs=vmem(),
        scratch_shapes=[
            pltpu.VMEM(weight.shape, BF),
            pltpu.VMEM((tokens, weight.shape[1]), BF),
            pltpu.VMEM((2, tokens, LANES), F32),
            pltpu.SemaphoreType.DMA((4,)),
        ],
        compiler_params=params(BIG),
        cost_estimate=cost(2 * weight.size * tokens, 2 * weight.size),
        name="backward",
    )(bal_cols, balance, resid, gain, weight, grad)


def weight_kernel(plan, depth, order_ref, gain_ref, scale_ref, grad_ref, *rest):
    count = len(plan)
    block_refs = rest[:-6]
    out_hbm, turned_ref, blocks_ref, result_ref, sems, out_sems = rest[-6:]
    tokens, features = block_refs[0].shape
    steps = features // depth
    inner = order_ref[count]

    def load(k, source):
        place = pl.ds(k * tokens, tokens)
        return pltpu.make_async_copy(block_refs[source], blocks_ref.at[place, :], sems.at[k])

    for k, choice in enumerate(plan):
        if len(choice) == 1:
            load(k, choice[0]).start()
        else:

            @pl.when(inner == 1)
            def _():
                load(k, choice[0]).start()

            @pl.when(inner == 0)
            def _():
                load(k, choice[1]).start()

    for k in range(count):
        turned_ref[:, k * tokens : (k + 1) * tokens] = grad_ref[order_ref[k], :tokens, :].T
    for k, choice in enumerate(plan):
        load(k, choice[0]).wait()

    def store(i):
        rows = pl.ds(pl.multiple_of(i * depth, depth), depth)
        return pltpu.make_async_copy(result_ref.at[rows, :], out_hbm.at[rows, :], out_sems.at[i])

    @pl.loop(0, steps)
    def _(i):
        part = pl.ds(pl.multiple_of(i * depth, depth), depth)
        value = jnp.dot(turned_ref[...], blocks_ref[:, part], preferred_element_type=F32)
        result_ref[part, :] = (value * gain_ref[:, part]).T * scale_ref[...]
        store(i).start()

    @pl.loop(0, steps)
    def _(i):
        store(i).wait()


def weight_grad(order, gain, col_scale, grads, blocks, plan):
    tokens, features = blocks[0].shape
    columns = grads.shape[2]
    depth = 512
    count = len(plan)
    return pl.pallas_call(
        functools.partial(weight_kernel, plan, depth),
        out_shape=jax.ShapeDtypeStruct((features, columns), F32),
        in_specs=[smem(), vmem(), vmem(), vmem()] + [hbm()] * len(blocks),
        out_specs=hbm(),
        scratch_shapes=[
            pltpu.VMEM((columns, tokens * count), BF),
            pltpu.VMEM((tokens * count, features), BF),
            pltpu.VMEM((features, columns), F32),
            pltpu.SemaphoreType.DMA((count,)),
            pltpu.SemaphoreType.DMA((features // depth,)),
        ],
        compiler_params=params(BIG),
        cost_estimate=cost(2 * tokens * count * features * columns, 8 * features * columns),
        name="weights",
    )(order, gain, col_scale, grads, *blocks)


def gather_blocks(resid):
    count = lax.axis_size("tok")
    place = lax.axis_index("tok")
    if count == 8:
        line, side = place // 2, place % 2

        def pairs(moves):
            return [(2 * a + s, 2 * b + s) for a, b in moves for s in range(2)]

        def cross(lines):
            return [(2 * a + s, 2 * a + 1 - s) for a in lines for s in range(2)]

        swap, out = pairs([(1, 2), (2, 1)]), pairs([(1, 0), (2, 3)])
        x0 = lax.ppermute(resid, "tok", cross(range(4)))
        z1 = lax.ppermute(resid, "tok", pairs([(0, 1), (1, 0), (2, 3), (3, 2)]))
        m1 = lax.ppermute(resid, "tok", swap)
        m2 = lax.ppermute(z1, "tok", swap)
        x1 = lax.ppermute(z1, "tok", cross(range(4)))
        f1 = lax.ppermute(m1, "tok", out)
        f2 = lax.ppermute(m2, "tok", out)
        x2m = lax.ppermute(m1, "tok", cross((1, 2)))
        x2e = lax.ppermute(f1, "tok", cross((0, 3)))
        x3m = lax.ppermute(m2, "tok", cross((1, 2)))
        x3e = lax.ppermute(f2, "tok", cross((0, 3)))
        low = line < 2
        inner = (line == 1) | (line == 2)
        lines = [line, line ^ 1, jnp.where(low, 2, 1), jnp.where(low, 3, 0)]
        order = [2 * a + (side ^ s) for a in lines for s in range(2)] + [inner.astype(jnp.int32)]
        blocks = [resid, x0, z1, x1, m1, f1, x2m, x2e, m2, f2, x3m, x3e]
        plan = ((0,), (1,), (2,), (3,), (4, 5), (6, 7), (8, 9), (10, 11))
        return blocks, jnp.stack(order), plan
    found = {0: resid}
    for flip in range(2, count, 2):
        found[flip] = exchange(resid, "tok", flip)
    for flip in range(0, count, 2):
        found[flip + 1] = exchange(found[flip], "tok", 1)
    order = jnp.append(place ^ jnp.arange(count), 0)
    return [found[flip] for flip in range(count)], order, tuple((flip,) for flip in range(count))


def total_over_tok(value):
    count = lax.axis_size("tok")
    flips = [1 << bit for bit in range(1, count.bit_length() - 1)] + [1] * (count > 1)
    for flip in flips:
        got = lax.ppermute(value, "tok", [(i, i ^ flip) for i in range(count)])
        value = value + got
    return value


def fast_device(resid, norm_gain, head_in, head_bias, head_out, targets, label_mask, obj_weight):
    tokens, features = resid.shape
    objectives, hidden = head_out.shape
    columns = objectives * hidden
    peers = lax.axis_size("tok")
    total_features = features * lax.axis_size("tp")
    total_tokens = tokens * peers
    me = lax.axis_index("tp")
    place = lax.axis_index("tok")
    gain = norm_gain[None, :]
    partner = [(i, i ^ 1) for i in range(4)]
    across = [(i, i ^ 2) for i in range(4)]

    blocks, order, plan = gather_blocks(resid)
    keep, send = forward((me % 2)[None], resid, gain, head_in)
    recv = lax.ppermute(send, "tp", partner)
    mine, send = merge((me // 2)[None], keep, recv)
    recv = lax.ppermute(send, "tp", across)
    gram = gram_of(head_in, objectives, hidden)
    part = heads(
        total_features,
        me[None],
        mine,
        recv,
        head_bias[None, :],
        head_out.reshape(1, columns),
        targets.T,
        label_mask.T,
    )
    part1 = lax.ppermute(part, "tp", partner)
    part2 = lax.ppermute(part, "tp", across)
    part3 = lax.ppermute(part2, "tp", partner)
    grad, message, col_sums = spread(me[None], (part, part1, part2, part3), gram, peers)
    grads = lax.all_to_all(message, "tok", 0, 0)
    along = products(resid, head_in, grad, objectives)
    squares = jnp.sum(grads[:, tokens : tokens + 3, :objectives].astype(F32), axis=(0, 1))
    squares = lax.psum(squares, "tp")
    obj_rms = jnp.sqrt(squares / (total_tokens * total_features) + grad_eps)
    balance = obj_weight.astype(F32) / denominator / obj_rms
    bal_cols = jnp.repeat(balance, hidden)
    gain_part = jnp.sum(balance[:, None] * along, axis=0, keepdims=True)
    sums = jnp.concatenate([gain_part, col_sums], axis=0)
    sums = total_over_tok(sums)
    resid_grad = backward(total_features, resid, gain, head_in, grad, bal_cols[None, :], balance[None, :])
    gain_grad = sums[0] / total_tokens
    head_bias_grad = sums[1] * bal_cols / total_tokens
    width = columns // peers
    col_scale = lax.dynamic_slice_in_dim(bal_cols, place * width, width, 0) / total_tokens
    head_in_grad = weight_grad(order, gain, col_scale[None, :], grads, blocks, plan)
    return (resid_grad, gain_grad, head_in_grad, head_bias_grad)


def head_gradient(preact, head_out, targets, label_mask):
    count = preact.shape[0]
    objectives, hidden = head_out.shape
    cube = preact.reshape(count, objectives, hidden)
    squash = jax.nn.sigmoid(cube)
    scores = jnp.sum(cube * squash * head_out[None], axis=2)
    errors = label_mask.astype(jnp.float32) * (scores - targets)
    slopes = squash * (1.0 + cube * (1.0 - squash))
    row_grad = (errors[:, :, None] * head_out[None] * slopes).astype(jnp.bfloat16)
    return row_grad.reshape(count, objectives * hidden)


def general_device(resid, norm_gain, head_in, head_bias, head_out, targets, label_mask, obj_weight):
    tok_rows = resid.shape[0]
    total_features = resid.shape[1] * lax.axis_size("tp")
    objectives, hidden = head_out.shape
    total_tokens = tok_rows * lax.axis_size("tok")
    floated = resid.astype(jnp.float32)
    row_sums = lax.psum(jnp.sum(floated * floated, axis=1), "tp")
    inverse = lax.rsqrt(row_sums[:, None] / total_features + norm_eps)
    unit = floated * inverse
    normed = (unit * norm_gain[None, :]).astype(jnp.bfloat16)
    partial_value = jnp.dot(normed, head_in, preferred_element_type=jnp.float32)
    quarter = lax.psum_scatter(partial_value, "tp", scatter_dimension=0, tiled=True)
    share = quarter.shape[0]
    offset = lax.axis_index("tp") * share
    part_targets = lax.dynamic_slice_in_dim(targets, offset, share, 0)
    part_mask = lax.dynamic_slice_in_dim(label_mask, offset, share, 0)
    part_grad = head_gradient(quarter + head_bias[None, :], head_out, part_targets, part_mask)
    row_grad = lax.all_gather(part_grad, "tp", axis=0, tiled=True)
    grad_float = row_grad.astype(jnp.float32)

    def objective_square(which):
        grad_slice = lax.dynamic_slice_in_dim(row_grad, which * hidden, hidden, 1)
        weight_slice = lax.dynamic_slice_in_dim(head_in, which * hidden, hidden, 1)
        feature_grad = lax.dot_general(
            grad_slice, weight_slice, (((1,), (1,)), ((), ())), preferred_element_type=jnp.float32
        )
        return jnp.sum(feature_grad * feature_grad)

    local_squares = lax.map(objective_square, jnp.arange(objectives))
    squares = lax.psum(local_squares, ("tok", "tp"))
    obj_rms = jnp.sqrt(squares / (total_tokens * total_features) + grad_eps)
    balance = obj_weight.astype(jnp.float32) / denominator / obj_rms
    balance_cols = jnp.repeat(balance, hidden)
    pre_grad = (grad_float * balance_cols[None, :]).astype(jnp.bfloat16)
    norm_grad = lax.dot_general(
        pre_grad, head_in, (((1,), (1,)), ((), ())), preferred_element_type=jnp.float32
    )
    gain_sum, bias_sum = lax.psum(
        (jnp.sum(norm_grad * unit, axis=0), jnp.sum(grad_float, axis=0)), "tok"
    )
    gain_grad = gain_sum / total_tokens
    head_bias_grad = bias_sum * balance_cols / total_tokens
    projection = lax.psum(jnp.sum(unit * norm_gain[None, :] * norm_grad, axis=1), "tp")
    resid_grad = (
        inverse * (norm_gain[None, :] * norm_grad - unit * (projection[:, None] / total_features))
    ).astype(jnp.bfloat16)
    weight_term = lax.dot_general(
        normed, row_grad, (((0,), (0,)), ((), ())), preferred_element_type=jnp.float32
    )
    summed_block = lax.psum_scatter(weight_term, "tok", scatter_dimension=1, tiled=True)
    columns = summed_block.shape[1]
    col_scale = lax.dynamic_slice_in_dim(balance_cols, lax.axis_index("tok") * columns, columns, 0)
    head_in_grad = summed_block * col_scale[None, :] / total_tokens
    return (resid_grad, gain_grad, head_in_grad, head_bias_grad)


def fits_fast(mesh, resid, head_in, head_out):
    peers, shards = mesh.shape["tok"], mesh.shape["tp"]
    columns = head_in.shape[1]
    tokens, features = resid.shape[0] // peers, resid.shape[1] // shards
    width = columns // peers
    fits = shards == 4 and peers & (peers - 1) == 0 and columns % peers == 0
    fits = fits and width % LANES == 0 and head_out.shape[1] == LANES and head_out.shape[0] <= 32
    return fits and tokens % 128 == 0 and features % 512 == 0 and columns % 1024 == 0


def solution(mesh):
    def mapped(body):
        return jax.shard_map(
            body,
            mesh=mesh,
            in_specs=(
                P("tok", "tp"),
                P("tp"),
                P("tp", None),
                P(),
                P(),
                P("tok", None),
                P("tok", None),
                P(),
            ),
            out_specs=(P("tok", "tp"), P("tp"), P("tp", "tok"), P()),
            check_vma=False,
        )


    def step(*args):
        if fits_fast(mesh, args[0], args[2], args[4]):
            return mapped(fast_device)(*args)
        return mapped(general_device)(*args)

    return step
```

```python
import functools

import jax
import jax.numpy as jnp
from jax import lax
from jax.experimental import pallas as pl
from jax.experimental.pallas import tpu as pltpu
from jax.sharding import PartitionSpec as P


norm_eps = 1e-05
grad_eps = 1e-06
denominator = 8.0
LANES = 128
BF = jnp.bfloat16
F32 = jnp.float32
MIB = 1 << 20
BIG = 50


def exchange(value, axis, flip):
    count = lax.axis_size(axis)
    return lax.ppermute(value, axis, [(i, i ^ flip) for i in range(count)])


def params(mib):
    return pltpu.CompilerParams(vmem_limit_bytes=mib * MIB)


def cost(flops, nbytes):
    return pl.CostEstimate(flops=int(flops), bytes_accessed=int(nbytes), transcendentals=0)


def vmem():
    return pl.BlockSpec(memory_space=pltpu.VMEM)


def fetch_columns(source, target, sems):
    width = target.shape[1] // sems.shape[0]

    def copy(i):
        part = pl.ds(pl.multiple_of(i * width, width), width)
        return pltpu.make_async_copy(source.at[:, part], target.at[:, part], sems.at[i])

    for i in range(sems.shape[0]):
        copy(i).start()
    return copy, width


def fetch_rows(source, target, sems):
    depth = target.shape[0] // sems.shape[0]

    def copy(i):
        part = pl.ds(pl.multiple_of(i * depth, depth), depth)
        return pltpu.make_async_copy(source.at[part, :], target.at[part, :], sems.at[i])

    for i in range(sems.shape[0]):
        copy(i).start()
    return copy, depth


def smem():
    return pl.BlockSpec(memory_space=pltpu.SMEM)


def hbm():
    return pl.BlockSpec(memory_space=pltpu.HBM)


def forward_kernel(core_ref, resid_ref, gain_ref, weight_hbm, keep_ref, send_ref, weight_ref, scaled_ref, sems):
    halves, rows, total = keep_ref.shape
    columns = total - LANES
    core = core_ref[0]
    copy, width = fetch_columns(weight_hbm, weight_ref, sems)

    def put(value, cols):
        for quarter in range(2 * halves):
            piece = value[quarter * rows : (quarter + 1) * rows]
            half = quarter // 2

            @pl.when(core == quarter % 2)
            def _():
                keep_ref[half, :, cols] = piece

            @pl.when(core != quarter % 2)
            def _():
                send_ref[half, :, cols] = piece

    floated = resid_ref[...].astype(F32)
    scaled_ref[...] = (floated * gain_ref[...]).astype(BF)
    sums = jnp.sum(floated * floated, axis=1, keepdims=True)
    put(jnp.broadcast_to(sums, (sums.shape[0], LANES)), pl.ds(columns, LANES))

    @pl.loop(0, sems.shape[0])
    def _(i):
        copy(i).wait()
        cols = pl.ds(pl.multiple_of(i * width, width), width)
        put(jnp.dot(scaled_ref[...], weight_ref[:, cols], preferred_element_type=F32), cols)


def forward(core, resid, gain, weight):
    tokens, features = resid.shape
    columns = weight.shape[1]
    out = jax.ShapeDtypeStruct((2, tokens // 4, columns + LANES), F32)
    return pl.pallas_call(
        forward_kernel,
        out_shape=(out, out),
        in_specs=[smem(), vmem(), vmem(), hbm()],
        out_specs=(vmem(), vmem()),
        scratch_shapes=[
            pltpu.VMEM(weight.shape, BF),
            pltpu.VMEM((tokens, features), BF),
            pltpu.SemaphoreType.DMA((4,)),
        ],
        compiler_params=params(BIG),
        cost_estimate=cost(2 * tokens * features * columns, 2 * features * columns),
        name="forward",
    )(core, resid, gain, weight)


def merge_kernel(side_ref, keep_ref, recv_ref, mine_ref, send_ref):
    side = side_ref[0]
    mine_ref[...] = keep_ref[side] + recv_ref[side]
    other = keep_ref[1 - side] + recv_ref[1 - side]
    columns = other.shape[1] - LANES
    send_ref[:, :columns] = other[:, :columns].astype(BF)
    tail = other[:, columns:]
    lane = lax.broadcasted_iota(jnp.int32, tail.shape, 1)
    high = tail.astype(BF).astype(F32)
    rest = tail - high
    middle = rest.astype(BF).astype(F32)
    send_ref[:, columns:] = jnp.where(lane == 0, high, jnp.where(lane == 1, middle, rest - middle)).astype(BF)


def merge(side, keep, recv):
    shape = keep.shape[1:]
    return pl.pallas_call(
        merge_kernel,
        out_shape=(jax.ShapeDtypeStruct(shape, F32), jax.ShapeDtypeStruct(shape, BF)),
        in_specs=[pl.BlockSpec(memory_space=pltpu.SMEM), vmem(), vmem()],
        out_specs=(vmem(), vmem()),
        compiler_params=params(8),
        cost_estimate=cost(keep.size, 3 * keep.size),
        name="merge",
    )(side, keep, recv)


def heads_kernel(
    features, me_ref, mine_ref, recv_ref, bias_ref, out_ref, targets_ref, mask_ref, msg_ref, turned_ref
):
    rows = mine_ref.shape[0]
    columns = mine_ref.shape[1] - LANES
    objectives = targets_ref.shape[0]
    hidden = columns // objectives
    start = pl.multiple_of(me_ref[0] * rows, rows)
    turned_ref[0] = targets_ref[...].T
    turned_ref[1] = mask_ref[...].astype(F32).T
    target = turned_ref[0, pl.ds(start, rows), :]
    mask = turned_ref[1, pl.ds(start, rows), :]
    tail = recv_ref[:, columns:].astype(F32)
    sums = mine_ref[:, columns : columns + 1] + ((tail[:, 0:1] + tail[:, 1:2]) + tail[:, 2:3])
    inverse = lax.rsqrt(sums / features + norm_eps)
    lane = lax.broadcasted_iota(jnp.int32, (rows, LANES), 1)
    extra = jnp.zeros((rows, LANES), F32)
    for which in range(objectives):
        cols = slice(which * hidden, (which + 1) * hidden)
        product = (mine_ref[:, cols] + recv_ref[:, cols].astype(F32)) * inverse
        value = product + bias_ref[:, cols]
        squash = jax.nn.sigmoid(value)
        weight = out_ref[:, cols]
        score = jnp.sum(value * squash * weight, axis=1, keepdims=True)
        error = mask[:, which : which + 1] * (score - target[:, which : which + 1])
        grad = (error * weight * (squash * (1.0 + value * (1.0 - squash)))).astype(BF)
        msg_ref[:, cols] = grad
        along = jnp.sum(grad.astype(F32) * product, axis=1, keepdims=True)
        high = along.astype(BF).astype(F32)
        extra = jnp.where(lane == which, high, extra)
        extra = jnp.where(lane == objectives + which, along - high, extra)
    high = inverse.astype(BF).astype(F32)
    rest = inverse - high
    middle = rest.astype(BF).astype(F32)
    extra = jnp.where(lane == 2 * objectives, high, extra)
    extra = jnp.where(lane == 2 * objectives + 1, middle, extra)
    extra = jnp.where(lane == 2 * objectives + 2, rest - middle, extra)
    msg_ref[:, columns:] = extra.astype(BF)


def heads(features, me, mine, recv, bias, head_out, targets, mask):
    tokens = targets.shape[1]
    return pl.pallas_call(
        functools.partial(heads_kernel, features),
        out_shape=jax.ShapeDtypeStruct(mine.shape, BF),
        in_specs=[pl.BlockSpec(memory_space=pltpu.SMEM)] + [vmem()] * 6,
        out_specs=vmem(),
        scratch_shapes=[pltpu.VMEM((2, tokens, targets.shape[0]), F32)],
        compiler_params=params(8),
        cost_estimate=cost(30 * mine.size, 8 * mine.size),
        name="heads",
    )(me, mine, recv, bias, head_out, targets, mask)


def scales(extra, objectives):
    extra = extra.astype(F32)
    at = 2 * objectives
    inverse = (extra[:, at : at + 1] + extra[:, at + 1 : at + 2]) + extra[:, at + 2 : at + 3]
    along = extra[:, :objectives] + extra[:, objectives:at]
    return inverse, along


def gram_kernel(weight_hbm, gram_ref, weight_ref, sems):
    objectives, hidden, _ = gram_ref.shape
    copy, width = fetch_columns(weight_hbm, weight_ref, sems)
    for which in range(objectives):
        if which * hidden % width == 0:
            copy(which * hidden // width).wait()
        block = weight_ref[:, which * hidden : (which + 1) * hidden]
        gram_ref[which] = lax.dot_general(block, block, (((0,), (0,)), ((), ())), preferred_element_type=F32)


def gram_of(weight, objectives, hidden):
    features, columns = weight.shape
    return pl.pallas_call(
        gram_kernel,
        out_shape=jax.ShapeDtypeStruct((objectives, hidden, hidden), F32),
        in_specs=[hbm()],
        out_specs=vmem(),
        scratch_shapes=[pltpu.VMEM(weight.shape, BF), pltpu.SemaphoreType.DMA((4,))],
        compiler_params=params(BIG),
        cost_estimate=cost(2 * features * columns * hidden, 2 * features * columns),
        name="gram",
    )(weight)


def spread_kernel(spot_ref, part0_ref, part1_ref, part2_ref, part3_ref, gram_ref, grad_ref, msg_ref, sums_ref):
    objectives, hidden, _ = gram_ref.shape
    peers, rows, width = msg_ref.shape
    tokens = grad_ref.shape[0]
    columns = objectives * hidden
    share = tokens // 4
    for flip, part_ref in enumerate((part0_ref, part1_ref, part2_ref, part3_ref)):
        start = pl.multiple_of((spot_ref[0] ^ flip) * share, share)
        grad_ref[pl.ds(start, share), :] = part_ref[...]
    inverse, _ = scales(grad_ref[:, columns:], objectives)
    lane = lax.broadcasted_iota(jnp.int32, (1, width), 1)
    squares = jnp.zeros((1, width), F32)
    for which in range(objectives):
        block = grad_ref[:, which * hidden : (which + 1) * hidden]
        pair = lax.dot_general(block, block, (((0,), (0,)), ((), ())), preferred_element_type=F32)
        total = jnp.sum(jnp.sum(pair * gram_ref[which], axis=0, keepdims=True), axis=1, keepdims=True)
        squares = jnp.where(lane == which, total, squares)
    for peer in range(peers):
        piece = grad_ref[:, peer * width : (peer + 1) * width].astype(F32)
        sums_ref[:, peer * width : (peer + 1) * width] = jnp.sum(piece, axis=0, keepdims=True)
        msg_ref[peer, :tokens, :] = (piece * inverse).astype(BF)
    high = squares.astype(BF).astype(F32)
    rest = squares - high
    middle = rest.astype(BF).astype(F32)
    row = lax.broadcasted_iota(jnp.int32, (rows - tokens, width), 0)
    tail = jnp.where(row == 0, high, jnp.where(row == 1, middle, jnp.where(row == 2, rest - middle, 0.0)))
    for peer in range(peers):
        msg_ref[peer, tokens:, :] = tail.astype(BF)


def spread(me, parts, gram, peers):
    share, total = parts[0].shape
    tokens = 4 * share
    columns = gram.shape[0] * gram.shape[1]
    return pl.pallas_call(
        spread_kernel,
        out_shape=(
            jax.ShapeDtypeStruct((tokens, total), BF),
            jax.ShapeDtypeStruct((peers, tokens + 16, columns // peers), BF),
            jax.ShapeDtypeStruct((1, columns), F32),
        ),
        in_specs=[pl.BlockSpec(memory_space=pltpu.SMEM)] + [vmem()] * 5,
        out_specs=(vmem(), vmem(), vmem()),
        compiler_params=params(16),
        cost_estimate=cost(2 * tokens * columns * gram.shape[1], 8 * tokens * total),
        name="spread",
    )(me, *parts, gram)


def products_kernel(resid_ref, weight_hbm, grad_ref, prod_hbm, along_ref, weight_ref, prod_ref, scal_ref, sems, out_sems):
    objectives = along_ref.shape[0]
    columns = weight_hbm.shape[1]
    hidden = columns // objectives
    copy, depth = fetch_rows(weight_hbm, weight_ref, sems)
    inverse, _ = scales(grad_ref[:, columns:], objectives)
    scal_ref[...] = jnp.broadcast_to(inverse, scal_ref.shape)

    def store(i):
        rows = pl.ds(pl.multiple_of(i * depth, depth), depth)
        return pltpu.make_async_copy(prod_ref.at[:, :, rows], prod_hbm.at[:, :, rows], out_sems.at[i])

    @pl.loop(0, sems.shape[0])
    def _(i):
        copy(i).wait()
        rows = pl.ds(pl.multiple_of(i * depth, depth), depth)
        unit = resid_ref[:, rows].astype(F32) * scal_ref[:, 0:1]
        for which in range(objectives):
            cols = slice(which * hidden, (which + 1) * hidden)
            value = lax.dot_general(
                grad_ref[:, cols], weight_ref[rows, cols], (((1,), (1,)), ((), ())), preferred_element_type=F32
            )
            along_ref[which : which + 1, rows] = jnp.sum(value * unit, axis=0, keepdims=True)
            prod_ref[which, :, rows] = value.astype(BF)
        store(i).start()

    @pl.loop(0, sems.shape[0])
    def _(i):
        store(i).wait()


def products(resid, weight, grad, objectives):
    tokens, features = resid.shape
    shape = (objectives, tokens, features)
    return pl.pallas_call(
        products_kernel,
        out_shape=(jax.ShapeDtypeStruct(shape, BF), jax.ShapeDtypeStruct((objectives, features), F32)),
        in_specs=[vmem(), hbm(), vmem()],
        out_specs=(hbm(), vmem()),
        scratch_shapes=[
            pltpu.VMEM(weight.shape, BF),
            pltpu.VMEM(shape, BF),
            pltpu.VMEM((tokens, LANES), F32),
            pltpu.SemaphoreType.DMA((4,)),
            pltpu.SemaphoreType.DMA((4,)),
        ],
        compiler_params=params(BIG),
        cost_estimate=cost(2 * weight.size * tokens, 4 * weight.size),
        name="products",
    )(resid, weight, grad)


def balance_kernel(entries, squares_ref, level_ref, along_ref, cols_ref, sums_ref, share_ref, wide_ref):
    objectives = along_ref.shape[0]
    hidden = wide_ref.shape[1] // objectives
    rms = jnp.sqrt(squares_ref[...] / entries + grad_eps)
    share = level_ref[...].astype(F32) / denominator / rms
    share_ref[...] = share
    row = lax.broadcasted_iota(jnp.int32, (objectives, objectives), 0)
    lane = lax.broadcasted_iota(jnp.int32, (objectives, objectives), 1)
    down = jnp.sum(jnp.where(row == lane, share, 0.0), axis=1, keepdims=True)
    sums_ref[0:1, :] = jnp.sum(along_ref[...] * down, axis=0, keepdims=True)
    sums_ref[1:2, :] = cols_ref[...]
    for which in range(objectives):
        wide_ref[:, which * hidden : (which + 1) * hidden] = jnp.broadcast_to(share[:, which : which + 1], (1, hidden))


def balance_of(entries, squares, level, along, col_sums):
    objectives, features = along.shape
    columns = col_sums.shape[1]
    return pl.pallas_call(
        functools.partial(balance_kernel, entries),
        out_shape=(
            jax.ShapeDtypeStruct((2, features), F32),
            jax.ShapeDtypeStruct((1, objectives), F32),
            jax.ShapeDtypeStruct((1, columns), F32),
        ),
        in_specs=[vmem()] * 4,
        out_specs=(vmem(), vmem(), vmem()),
        compiler_params=params(4),
        cost_estimate=cost(4 * along.size, 8 * along.size),
        name="balance",
    )(squares, level, along, col_sums)


def backward_kernel(total, share_ref, row_ref, resid_ref, gain_ref, prod_hbm, extra_ref, out_ref, prod_ref, scal_ref, sems):
    objectives, _, features = prod_hbm.shape
    chunks = sems.shape[0]
    depth = features // chunks

    def copy(i):
        part = pl.ds(pl.multiple_of(i * depth, depth), depth)
        return pltpu.make_async_copy(prod_hbm.at[:, :, part], prod_ref.at[:, :, part], sems.at[i])

    for i in range(chunks):
        copy(i).start()
    inverse, along = scales(extra_ref[...], objectives)
    projection = jnp.sum(along * row_ref[...], axis=1, keepdims=True) / total
    scal_ref[0] = jnp.broadcast_to(inverse, scal_ref.shape[1:])
    scal_ref[1] = jnp.broadcast_to(projection, scal_ref.shape[1:])

    @pl.loop(0, chunks)
    def _(i):
        copy(i).wait()

        @pl.loop(0, depth // LANES)
        def _(k):
            part = pl.ds(pl.multiple_of(i * depth + k * LANES, LANES), LANES)
            grad = prod_ref[0, :, part].astype(F32) * share_ref[0, 0]
            for which in range(1, objectives):
                grad += prod_ref[which, :, part].astype(F32) * share_ref[0, which]
            inverse = scal_ref[0]
            unit = resid_ref[:, part].astype(F32) * inverse
            out_ref[:, part] = (inverse * (gain_ref[:, part] * grad - unit * scal_ref[1])).astype(BF)


def backward(total, resid, gain, prods, grad, share):
    tokens, _ = resid.shape
    tail = grad.shape[1] // LANES - 1
    whole = lambda array: pl.BlockSpec(array.shape, lambda i: (0,) * array.ndim)
    return pl.pallas_call(
        functools.partial(backward_kernel, total),
        out_shape=jax.ShapeDtypeStruct(resid.shape, BF),
        grid=(1,),
        in_specs=[
            smem(),
            whole(share),
            whole(resid),
            whole(gain),
            hbm(),
            pl.BlockSpec((tokens, LANES), lambda i: (0, tail)),
        ],
        out_specs=whole(resid),
        scratch_shapes=[
            pltpu.VMEM(prods.shape, BF),
            pltpu.VMEM((2, tokens, LANES), F32),
            pltpu.SemaphoreType.DMA((4,)),
        ],
        compiler_params=params(BIG),
        cost_estimate=cost(2 * prods.size, 2 * prods.size),
        name="backward",
    )(share, share, resid, gain, prods, grad)


def weight_kernel(plan, order_of, depth, place_ref, gain_ref, wide_ref, sum_ref, got_ref, grad_ref, *rest):
    count = len(plan)
    block_refs = rest[:-8]
    out_hbm, gain_out_ref, bias_out_ref, turned_ref, blocks_ref, result_ref, sems, out_sems = rest[-8:]
    tokens, features = block_refs[0].shape
    columns = grad_ref.shape[2]
    total_tokens = tokens * count
    order, inner = order_of(place_ref[0])
    chunks = sems.shape[1]
    width = features // chunks

    def load(k, source, i):
        place = (pl.ds(k * tokens, tokens), pl.ds(i * width, width))
        return pltpu.make_async_copy(block_refs[source].at[:, place[1]], blocks_ref.at[place], sems.at[k, i])

    for i in range(chunks):
        for k, choice in enumerate(plan):
            if len(choice) == 1:
                load(k, choice[0], i).start()
            else:

                @pl.when(inner == 1)
                def _():
                    load(k, choice[0], i).start()

                @pl.when(inner == 0)
                def _():
                    load(k, choice[1], i).start()

    for k in range(count):
        turned_ref[:, k * tokens : (k + 1) * tokens] = grad_ref[order[k], :tokens, :].T
    sums = (sum_ref[...] + got_ref[...]) / total_tokens
    gain_out_ref[...] = sums[0:1]
    bias_out_ref[...] = sums[1:2] * wide_ref[...]
    start = pl.multiple_of(place_ref[0] * columns, columns)
    scale = wide_ref[:, pl.ds(start, columns)] / total_tokens

    def store(i):
        rows = pl.ds(pl.multiple_of(i * depth, depth), depth)
        return pltpu.make_async_copy(result_ref.at[rows, :], out_hbm.at[rows, :], out_sems.at[i])

    for i in range(chunks):
        for k, choice in enumerate(plan):
            load(k, choice[0], i).wait()

        @pl.loop(i * width // depth, (i + 1) * width // depth)
        def _(step):
            part = pl.ds(pl.multiple_of(step * depth, depth), depth)
            value = jnp.dot(turned_ref[...], blocks_ref[:, part], preferred_element_type=F32)
            result_ref[part, :] = (value * gain_ref[:, part]).T * scale
            store(step).start()

    @pl.loop(0, features // depth)
    def _(step):
        store(step).wait()


def weight_grad(place, gain, wide, sums, got, grads, blocks, plan, order_of):
    tokens, features = blocks[0].shape
    columns = grads.shape[2]
    depth = 512
    count = len(plan)
    return pl.pallas_call(
        functools.partial(weight_kernel, plan, order_of, depth),
        out_shape=(
            jax.ShapeDtypeStruct((features, columns), F32),
            jax.ShapeDtypeStruct((1, features), F32),
            jax.ShapeDtypeStruct(wide.shape, F32),
        ),
        in_specs=[smem()] + [vmem()] * 5 + [hbm()] * len(blocks),
        out_specs=(hbm(), vmem(), vmem()),
        scratch_shapes=[
            pltpu.VMEM((columns, tokens * count), BF),
            pltpu.VMEM((tokens * count, features), BF),
            pltpu.VMEM((features, columns), F32),
            pltpu.SemaphoreType.DMA((count, 2)),
            pltpu.SemaphoreType.DMA((features // depth,)),
        ],
        compiler_params=params(BIG),
        cost_estimate=cost(2 * tokens * count * features * columns, 8 * features * columns),
        name="weights",
    )(place, gain, wide, sums, got, grads, *blocks)


def gather_blocks(resid):
    count = lax.axis_size("tok")
    if count == 8:

        def pairs(moves):
            return [(2 * a + s, 2 * b + s) for a, b in moves for s in range(2)]

        def cross(lines):
            return [(2 * a + s, 2 * a + 1 - s) for a in lines for s in range(2)]

        swap, out = pairs([(1, 2), (2, 1)]), pairs([(1, 0), (2, 3)])
        x0 = lax.ppermute(resid, "tok", cross(range(4)))
        z1 = lax.ppermute(resid, "tok", pairs([(0, 1), (1, 0), (2, 3), (3, 2)]))
        m1 = lax.ppermute(resid, "tok", swap)
        m2 = lax.ppermute(z1, "tok", swap)
        x1 = lax.ppermute(z1, "tok", cross(range(4)))
        f1 = lax.ppermute(m1, "tok", out)
        f2 = lax.ppermute(m2, "tok", out)
        x2m = lax.ppermute(m1, "tok", cross((1, 2)))
        x2e = lax.ppermute(f1, "tok", cross((0, 3)))
        x3m = lax.ppermute(m2, "tok", cross((1, 2)))
        x3e = lax.ppermute(f2, "tok", cross((0, 3)))

        def order_of(place):
            line, side = place // 2, place % 2
            low = line < 2
            inner = jnp.where((line == 1) | (line == 2), 1, 0)
            lines = [line, jnp.where(line % 2 == 0, line + 1, line - 1), jnp.where(low, 2, 1), jnp.where(low, 3, 0)]
            return [2 * a + s for a in lines for s in (side, 1 - side)], inner

        blocks = [resid, x0, z1, x1, m1, f1, x2m, x2e, m2, f2, x3m, x3e]
        plan = ((0,), (1,), (2,), (3,), (4, 5), (6, 7), (8, 9), (10, 11))
        return blocks, plan, order_of
    found = {0: resid}
    for flip in range(2, count, 2):
        found[flip] = exchange(resid, "tok", flip)
    for flip in range(0, count, 2):
        found[flip + 1] = exchange(found[flip], "tok", 1)
    plan = tuple((flip,) for flip in range(count))
    return [found[flip] for flip in range(count)], plan, lambda place: ([place ^ flip for flip in range(count)], 0)


def total_over_tok(value):
    count = lax.axis_size("tok")
    flips = [1 << bit for bit in range(1, count.bit_length() - 1)] + [1]
    got = None
    for step, flip in enumerate(flips):
        if step:
            value = value + got
        got = lax.ppermute(value, "tok", [(i, i ^ flip) for i in range(count)])
    return value, got


def fast_device(resid, norm_gain, head_in, head_bias, head_out, targets, label_mask, obj_weight):
    tokens, features = resid.shape
    objectives, hidden = head_out.shape
    columns = objectives * hidden
    peers = lax.axis_size("tok")
    total_features = features * lax.axis_size("tp")
    total_tokens = tokens * peers
    me = lax.axis_index("tp")
    place = lax.axis_index("tok")
    gain = norm_gain[None, :]
    partner = [(i, i ^ 1) for i in range(4)]
    across = [(i, i ^ 2) for i in range(4)]

    blocks, plan, order_of = gather_blocks(resid)
    keep, send = forward((me % 2)[None], resid, gain, head_in)
    recv = lax.ppermute(send, "tp", partner)
    mine, send = merge((me // 2)[None], keep, recv)
    recv = lax.ppermute(send, "tp", across)
    gram = gram_of(head_in, objectives, hidden)
    part = heads(
        total_features,
        me[None],
        mine,
        recv,
        head_bias[None, :],
        head_out.reshape(1, columns),
        targets.T,
        label_mask.T,
    )
    part1 = lax.ppermute(part, "tp", partner)
    part2 = lax.ppermute(part, "tp", across)
    part3 = lax.ppermute(part2, "tp", partner)
    grad, message, col_sums = spread(me[None], (part, part1, part2, part3), gram, peers)
    grads = lax.all_to_all(message, "tok", 0, 0)
    prods, along = products(resid, head_in, grad, objectives)
    squares = jnp.sum(grads[:, tokens : tokens + 3, :objectives].astype(F32), axis=(0, 1))
    squares = lax.psum(squares, "tp")[None, :]
    entries = total_tokens * total_features
    sums, share, wide = balance_of(entries, squares, obj_weight[None, :], along, col_sums)
    sums, got = total_over_tok(sums)
    resid_grad = backward(total_features, resid, gain, prods, grad, share)
    head_in_grad, gain_grad, head_bias_grad = weight_grad(
        place[None], gain, wide, sums, got, grads, blocks, plan, order_of
    )
    return (resid_grad, gain_grad[0], head_in_grad, head_bias_grad[0])


def head_gradient(preact, head_out, targets, label_mask):
    count = preact.shape[0]
    objectives, hidden = head_out.shape
    cube = preact.reshape(count, objectives, hidden)
    squash = jax.nn.sigmoid(cube)
    scores = jnp.sum(cube * squash * head_out[None], axis=2)
    errors = label_mask.astype(jnp.float32) * (scores - targets)
    slopes = squash * (1.0 + cube * (1.0 - squash))
    row_grad = (errors[:, :, None] * head_out[None] * slopes).astype(jnp.bfloat16)
    return row_grad.reshape(count, objectives * hidden)


def general_device(resid, norm_gain, head_in, head_bias, head_out, targets, label_mask, obj_weight):
    tok_rows = resid.shape[0]
    total_features = resid.shape[1] * lax.axis_size("tp")
    objectives, hidden = head_out.shape
    total_tokens = tok_rows * lax.axis_size("tok")
    floated = resid.astype(jnp.float32)
    row_sums = lax.psum(jnp.sum(floated * floated, axis=1), "tp")
    inverse = lax.rsqrt(row_sums[:, None] / total_features + norm_eps)
    unit = floated * inverse
    normed = (unit * norm_gain[None, :]).astype(jnp.bfloat16)
    partial_value = jnp.dot(normed, head_in, preferred_element_type=jnp.float32)
    quarter = lax.psum_scatter(partial_value, "tp", scatter_dimension=0, tiled=True)
    share = quarter.shape[0]
    offset = lax.axis_index("tp") * share
    part_targets = lax.dynamic_slice_in_dim(targets, offset, share, 0)
    part_mask = lax.dynamic_slice_in_dim(label_mask, offset, share, 0)
    part_grad = head_gradient(quarter + head_bias[None, :], head_out, part_targets, part_mask)
    row_grad = lax.all_gather(part_grad, "tp", axis=0, tiled=True)
    grad_float = row_grad.astype(jnp.float32)

    def objective_square(which):
        grad_slice = lax.dynamic_slice_in_dim(row_grad, which * hidden, hidden, 1)
        weight_slice = lax.dynamic_slice_in_dim(head_in, which * hidden, hidden, 1)
        feature_grad = lax.dot_general(
            grad_slice, weight_slice, (((1,), (1,)), ((), ())), preferred_element_type=jnp.float32
        )
        return jnp.sum(feature_grad * feature_grad)

    local_squares = lax.map(objective_square, jnp.arange(objectives))
    squares = lax.psum(local_squares, ("tok", "tp"))
    obj_rms = jnp.sqrt(squares / (total_tokens * total_features) + grad_eps)
    balance = obj_weight.astype(jnp.float32) / denominator / obj_rms
    balance_cols = jnp.repeat(balance, hidden)
    pre_grad = (grad_float * balance_cols[None, :]).astype(jnp.bfloat16)
    norm_grad = lax.dot_general(
        pre_grad, head_in, (((1,), (1,)), ((), ())), preferred_element_type=jnp.float32
    )
    gain_sum, bias_sum = lax.psum(
        (jnp.sum(norm_grad * unit, axis=0), jnp.sum(grad_float, axis=0)), "tok"
    )
    gain_grad = gain_sum / total_tokens
    head_bias_grad = bias_sum * balance_cols / total_tokens
    projection = lax.psum(jnp.sum(unit * norm_gain[None, :] * norm_grad, axis=1), "tp")
    resid_grad = (
        inverse * (norm_gain[None, :] * norm_grad - unit * (projection[:, None] / total_features))
    ).astype(jnp.bfloat16)
    weight_term = lax.dot_general(
        normed, row_grad, (((0,), (0,)), ((), ())), preferred_element_type=jnp.float32
    )
    summed_block = lax.psum_scatter(weight_term, "tok", scatter_dimension=1, tiled=True)
    columns = summed_block.shape[1]
    col_scale = lax.dynamic_slice_in_dim(balance_cols, lax.axis_index("tok") * columns, columns, 0)
    head_in_grad = summed_block * col_scale[None, :] / total_tokens
    return (resid_grad, gain_grad, head_in_grad, head_bias_grad)


def fits_fast(mesh, resid, head_in, head_out):
    peers, shards = mesh.shape["tok"], mesh.shape["tp"]
    columns = head_in.shape[1]
    tokens, features = resid.shape[0] // peers, resid.shape[1] // shards
    width = columns // peers
    fits = shards == 4 and peers & (peers - 1) == 0 and columns % peers == 0
    fits = fits and peers > 1 and width % LANES == 0 and head_out.shape[1] == LANES and head_out.shape[0] <= 32
    return fits and tokens % 128 == 0 and features % 512 == 0 and columns % 1024 == 0


def solution(mesh):
    def mapped(body):
        return jax.shard_map(
            body,
            mesh=mesh,
            in_specs=(
                P("tok", "tp"),
                P("tp"),
                P("tp", None),
                P(),
                P(),
                P("tok", None),
                P("tok", None),
                P(),
            ),
            out_specs=(P("tok", "tp"), P("tp"), P("tp", "tok"), P()),
            check_vma=False,
        )


    def step(*args):
        if fits_fast(mesh, args[0], args[2], args[4]):
            return mapped(fast_device)(*args)
        return mapped(general_device)(*args)

    return step
```

```python
import functools

import jax
import jax.numpy as jnp
from jax import lax
from jax.experimental import pallas as pl
from jax.experimental.pallas import tpu as pltpu
from jax.sharding import PartitionSpec as P


norm_eps = 1e-05
grad_eps = 1e-06
denominator = 8.0
LANES = 128
BF = jnp.bfloat16
F32 = jnp.float32
MIB = 1 << 20
BIG = 50


def exchange(value, axis, flip):
    count = lax.axis_size(axis)
    return lax.ppermute(value, axis, [(i, i ^ flip) for i in range(count)])


def params(mib):
    return pltpu.CompilerParams(vmem_limit_bytes=mib * MIB)


def cost(flops, nbytes):
    return pl.CostEstimate(flops=int(flops), bytes_accessed=int(nbytes), transcendentals=0)


def vmem():
    return pl.BlockSpec(memory_space=pltpu.VMEM)


def fetch_columns(source, target, sems):
    width = target.shape[1] // sems.shape[0]

    def copy(i):
        part = pl.ds(pl.multiple_of(i * width, width), width)
        return pltpu.make_async_copy(source.at[:, part], target.at[:, part], sems.at[i])

    for i in range(sems.shape[0]):
        copy(i).start()
    return copy, width


def fetch_rows(source, target, sems):
    depth = target.shape[0] // sems.shape[0]

    def copy(i):
        part = pl.ds(pl.multiple_of(i * depth, depth), depth)
        return pltpu.make_async_copy(source.at[part, :], target.at[part, :], sems.at[i])

    for i in range(sems.shape[0]):
        copy(i).start()
    return copy, depth


def smem():
    return pl.BlockSpec(memory_space=pltpu.SMEM)


def hbm():
    return pl.BlockSpec(memory_space=pltpu.HBM)


def forward_kernel(
    core_ref, resid_hbm, gain_hbm, weight_hbm, keep_ref, send_ref, weight_ref, resid_ref, gain_ref, scaled_ref, sems, own_sems
):
    halves, rows, total = keep_ref.shape
    columns = total - LANES
    core = core_ref[0]
    own = [
        pltpu.make_async_copy(resid_hbm, resid_ref, own_sems.at[0]),
        pltpu.make_async_copy(gain_hbm, gain_ref, own_sems.at[1]),
    ]
    for one in own:
        one.start()
    copy, width = fetch_columns(weight_hbm, weight_ref, sems)

    def put(value, cols):
        for quarter in range(2 * halves):
            piece = value[quarter * rows : (quarter + 1) * rows]
            half = quarter // 2

            @pl.when(core == quarter % 2)
            def _():
                keep_ref[half, :, cols] = piece

            @pl.when(core != quarter % 2)
            def _():
                send_ref[half, :, cols] = piece

    for one in own:
        one.wait()
    floated = resid_ref[...].astype(F32)
    scaled_ref[...] = (floated * gain_ref[...]).astype(BF)
    sums = jnp.sum(floated * floated, axis=1, keepdims=True)
    put(jnp.broadcast_to(sums, (sums.shape[0], LANES)), pl.ds(columns, LANES))

    @pl.loop(0, sems.shape[0])
    def _(i):
        copy(i).wait()
        cols = pl.ds(pl.multiple_of(i * width, width), width)
        put(jnp.dot(scaled_ref[...], weight_ref[:, cols], preferred_element_type=F32), cols)


def forward(core, resid, gain, weight):
    tokens, features = resid.shape
    columns = weight.shape[1]
    out = jax.ShapeDtypeStruct((2, tokens // 4, columns + LANES), F32)
    return pl.pallas_call(
        forward_kernel,
        out_shape=(out, out),
        in_specs=[smem(), hbm(), hbm(), hbm()],
        out_specs=(vmem(), vmem()),
        scratch_shapes=[
            pltpu.VMEM(weight.shape, BF),
            pltpu.VMEM((tokens, features), BF),
            pltpu.VMEM((1, features), F32),
            pltpu.VMEM((tokens, features), BF),
            pltpu.SemaphoreType.DMA((4,)),
            pltpu.SemaphoreType.DMA((2,)),
        ],
        compiler_params=params(BIG),
        cost_estimate=cost(2 * tokens * features * columns, 2 * features * columns),
        name="forward",
    )(core, resid, gain, weight)


def merge_kernel(side_ref, keep_ref, recv_ref, mine_ref, send_ref):
    side = side_ref[0]
    mine_ref[...] = keep_ref[side] + recv_ref[side]
    other = keep_ref[1 - side] + recv_ref[1 - side]
    columns = other.shape[1] - LANES
    send_ref[:, :columns] = other[:, :columns].astype(BF)
    tail = other[:, columns:]
    lane = lax.broadcasted_iota(jnp.int32, tail.shape, 1)
    high = tail.astype(BF).astype(F32)
    rest = tail - high
    middle = rest.astype(BF).astype(F32)
    send_ref[:, columns:] = jnp.where(lane == 0, high, jnp.where(lane == 1, middle, rest - middle)).astype(BF)


def merge(side, keep, recv):
    shape = keep.shape[1:]
    return pl.pallas_call(
        merge_kernel,
        out_shape=(jax.ShapeDtypeStruct(shape, F32), jax.ShapeDtypeStruct(shape, BF)),
        in_specs=[pl.BlockSpec(memory_space=pltpu.SMEM), vmem(), vmem()],
        out_specs=(vmem(), vmem()),
        compiler_params=params(8),
        cost_estimate=cost(keep.size, 3 * keep.size),
        name="merge",
    )(side, keep, recv)


def heads_kernel(
    features, me_ref, mine_ref, recv_ref, bias_ref, out_ref, targets_ref, mask_ref, msg_ref, turned_ref
):
    rows = mine_ref.shape[0]
    columns = mine_ref.shape[1] - LANES
    objectives = targets_ref.shape[0]
    hidden = columns // objectives
    start = pl.multiple_of(me_ref[0] * rows, rows)
    turned_ref[0] = targets_ref[...].T
    turned_ref[1] = mask_ref[...].astype(F32).T
    target = turned_ref[0, pl.ds(start, rows), :]
    mask = turned_ref[1, pl.ds(start, rows), :]
    tail = recv_ref[:, columns:].astype(F32)
    sums = mine_ref[:, columns : columns + 1] + ((tail[:, 0:1] + tail[:, 1:2]) + tail[:, 2:3])
    inverse = lax.rsqrt(sums / features + norm_eps)
    lane = lax.broadcasted_iota(jnp.int32, (rows, LANES), 1)
    extra = jnp.zeros((rows, LANES), F32)
    for which in range(objectives):
        cols = slice(which * hidden, (which + 1) * hidden)
        product = (mine_ref[:, cols] + recv_ref[:, cols].astype(F32)) * inverse
        value = product + bias_ref[:, cols]
        squash = jax.nn.sigmoid(value)
        weight = out_ref[:, cols]
        score = jnp.sum(value * squash * weight, axis=1, keepdims=True)
        error = mask[:, which : which + 1] * (score - target[:, which : which + 1])
        grad = (error * weight * (squash * (1.0 + value * (1.0 - squash)))).astype(BF)
        msg_ref[:, cols] = grad
        along = jnp.sum(grad.astype(F32) * product, axis=1, keepdims=True)
        high = along.astype(BF).astype(F32)
        extra = jnp.where(lane == which, high, extra)
        extra = jnp.where(lane == objectives + which, along - high, extra)
    high = inverse.astype(BF).astype(F32)
    rest = inverse - high
    middle = rest.astype(BF).astype(F32)
    extra = jnp.where(lane == 2 * objectives, high, extra)
    extra = jnp.where(lane == 2 * objectives + 1, middle, extra)
    extra = jnp.where(lane == 2 * objectives + 2, rest - middle, extra)
    msg_ref[:, columns:] = extra.astype(BF)


def heads(features, me, mine, recv, bias, head_out, targets, mask):
    tokens = targets.shape[1]
    return pl.pallas_call(
        functools.partial(heads_kernel, features),
        out_shape=jax.ShapeDtypeStruct(mine.shape, BF),
        in_specs=[pl.BlockSpec(memory_space=pltpu.SMEM)] + [vmem()] * 6,
        out_specs=vmem(),
        scratch_shapes=[pltpu.VMEM((2, tokens, targets.shape[0]), F32)],
        compiler_params=params(8),
        cost_estimate=cost(30 * mine.size, 8 * mine.size),
        name="heads",
    )(me, mine, recv, bias, head_out, targets, mask)


def scales(extra, objectives):
    extra = extra.astype(F32)
    at = 2 * objectives
    inverse = (extra[:, at : at + 1] + extra[:, at + 1 : at + 2]) + extra[:, at + 2 : at + 3]
    along = extra[:, :objectives] + extra[:, objectives:at]
    return inverse, along


def gram_kernel(weight_hbm, gram_ref, weight_ref, sems):
    objectives, hidden, _ = gram_ref.shape
    copy, width = fetch_columns(weight_hbm, weight_ref, sems)
    for which in range(objectives):
        if which * hidden % width == 0:
            copy(which * hidden // width).wait()
        block = weight_ref[:, which * hidden : (which + 1) * hidden]
        gram_ref[which] = lax.dot_general(block, block, (((0,), (0,)), ((), ())), preferred_element_type=F32)


def gram_of(weight, objectives, hidden):
    features, columns = weight.shape
    return pl.pallas_call(
        gram_kernel,
        out_shape=jax.ShapeDtypeStruct((objectives, hidden, hidden), F32),
        in_specs=[hbm()],
        out_specs=vmem(),
        scratch_shapes=[pltpu.VMEM(weight.shape, BF), pltpu.SemaphoreType.DMA((4,))],
        compiler_params=params(BIG),
        cost_estimate=cost(2 * features * columns * hidden, 2 * features * columns),
        name="gram",
    )(weight)


def spread_kernel(spot_ref, part0_ref, part1_ref, part2_ref, part3_ref, gram_ref, grad_ref, msg_ref, sums_ref):
    objectives, hidden, _ = gram_ref.shape
    peers, rows, width = msg_ref.shape
    tokens = grad_ref.shape[0]
    columns = objectives * hidden
    share = tokens // 4
    for flip, part_ref in enumerate((part0_ref, part1_ref, part2_ref, part3_ref)):
        start = pl.multiple_of((spot_ref[0] ^ flip) * share, share)
        grad_ref[pl.ds(start, share), :] = part_ref[...]
    inverse, _ = scales(grad_ref[:, columns:], objectives)
    lane = lax.broadcasted_iota(jnp.int32, (1, width), 1)
    squares = jnp.zeros((1, width), F32)
    for which in range(objectives):
        block = grad_ref[:, which * hidden : (which + 1) * hidden]
        pair = lax.dot_general(block, block, (((0,), (0,)), ((), ())), preferred_element_type=F32)
        total = jnp.sum(jnp.sum(pair * gram_ref[which], axis=0, keepdims=True), axis=1, keepdims=True)
        squares = jnp.where(lane == which, total, squares)
    for peer in range(peers):
        piece = grad_ref[:, peer * width : (peer + 1) * width].astype(F32)
        sums_ref[:, peer * width : (peer + 1) * width] = jnp.sum(piece, axis=0, keepdims=True)
        msg_ref[peer, :tokens, :] = (piece * inverse).astype(BF)
    high = squares.astype(BF).astype(F32)
    rest = squares - high
    middle = rest.astype(BF).astype(F32)
    row = lax.broadcasted_iota(jnp.int32, (rows - tokens, width), 0)
    tail = jnp.where(row == 0, high, jnp.where(row == 1, middle, jnp.where(row == 2, rest - middle, 0.0)))
    for peer in range(peers):
        msg_ref[peer, tokens:, :] = tail.astype(BF)


def spread(me, parts, gram, peers):
    share, total = parts[0].shape
    tokens = 4 * share
    columns = gram.shape[0] * gram.shape[1]
    return pl.pallas_call(
        spread_kernel,
        out_shape=(
            jax.ShapeDtypeStruct((tokens, total), BF),
            jax.ShapeDtypeStruct((peers, tokens + 16, columns // peers), BF),
            jax.ShapeDtypeStruct((1, columns), F32),
        ),
        in_specs=[pl.BlockSpec(memory_space=pltpu.SMEM)] + [vmem()] * 5,
        out_specs=(vmem(), vmem(), vmem()),
        compiler_params=params(16),
        cost_estimate=cost(2 * tokens * columns * gram.shape[1], 8 * tokens * total),
        name="spread",
    )(me, *parts, gram)


def products_kernel(resid_ref, weight_hbm, grad_ref, prod_hbm, along_ref, weight_ref, prod_ref, scal_ref, sems, out_sems):
    objectives = along_ref.shape[0]
    columns = weight_hbm.shape[1]
    hidden = columns // objectives
    copy, depth = fetch_rows(weight_hbm, weight_ref, sems)
    inverse, _ = scales(grad_ref[:, columns:], objectives)
    scal_ref[...] = jnp.broadcast_to(inverse, scal_ref.shape)

    def store(i):
        rows = pl.ds(pl.multiple_of(i * depth, depth), depth)
        return pltpu.make_async_copy(prod_ref.at[:, :, rows], prod_hbm.at[:, :, rows], out_sems.at[i])

    @pl.loop(0, sems.shape[0])
    def _(i):
        copy(i).wait()
        rows = pl.ds(pl.multiple_of(i * depth, depth), depth)
        unit = resid_ref[:, rows].astype(F32) * scal_ref[:, 0:1]
        for which in range(objectives):
            cols = slice(which * hidden, (which + 1) * hidden)
            value = lax.dot_general(
                grad_ref[:, cols], weight_ref[rows, cols], (((1,), (1,)), ((), ())), preferred_element_type=F32
            )
            along_ref[which : which + 1, rows] = jnp.sum(value * unit, axis=0, keepdims=True)
            prod_ref[which, :, rows] = value.astype(BF)
        store(i).start()

    @pl.loop(0, sems.shape[0])
    def _(i):
        store(i).wait()


def products(resid, weight, grad, objectives):
    tokens, features = resid.shape
    shape = (objectives, tokens, features)
    return pl.pallas_call(
        products_kernel,
        out_shape=(jax.ShapeDtypeStruct(shape, BF), jax.ShapeDtypeStruct((objectives, features), F32)),
        in_specs=[vmem(), hbm(), vmem()],
        out_specs=(hbm(), vmem()),
        scratch_shapes=[
            pltpu.VMEM(weight.shape, BF),
            pltpu.VMEM(shape, BF),
            pltpu.VMEM((tokens, LANES), F32),
            pltpu.SemaphoreType.DMA((4,)),
            pltpu.SemaphoreType.DMA((4,)),
        ],
        compiler_params=params(BIG),
        cost_estimate=cost(2 * weight.size * tokens, 4 * weight.size),
        name="products",
    )(resid, weight, grad)


def balance_kernel(entries, squares_ref, got_ref, level_ref, along_ref, cols_ref, sums_ref, share_ref, wide_ref):
    objectives = along_ref.shape[0]
    hidden = wide_ref.shape[1] // objectives
    rms = jnp.sqrt((squares_ref[...] + got_ref[...]) / entries + grad_eps)
    share = level_ref[...].astype(F32) / denominator / rms
    share_ref[...] = share
    row = lax.broadcasted_iota(jnp.int32, (objectives, objectives), 0)
    lane = lax.broadcasted_iota(jnp.int32, (objectives, objectives), 1)
    down = jnp.sum(jnp.where(row == lane, share, 0.0), axis=1, keepdims=True)
    sums_ref[0:1, :] = jnp.sum(along_ref[...] * down, axis=0, keepdims=True)
    sums_ref[1:2, :] = cols_ref[...]
    for which in range(objectives):
        wide_ref[:, which * hidden : (which + 1) * hidden] = jnp.broadcast_to(share[:, which : which + 1], (1, hidden))


def balance_of(entries, squares, got, level, along, col_sums):
    objectives, features = along.shape
    columns = col_sums.shape[1]
    return pl.pallas_call(
        functools.partial(balance_kernel, entries),
        out_shape=(
            jax.ShapeDtypeStruct((2, features), F32),
            jax.ShapeDtypeStruct((1, objectives), F32),
            jax.ShapeDtypeStruct((1, columns), F32),
        ),
        in_specs=[vmem()] * 5,
        out_specs=(vmem(), vmem(), vmem()),
        compiler_params=params(4),
        cost_estimate=cost(4 * along.size, 8 * along.size),
        name="balance",
    )(squares, got, level, along, col_sums)


def backward_kernel(total, share_ref, row_ref, resid_ref, gain_ref, prod_hbm, extra_ref, out_ref, prod_ref, scal_ref, sems):
    objectives, _, features = prod_hbm.shape
    chunks = sems.shape[0]
    depth = features // chunks

    def copy(i):
        part = pl.ds(pl.multiple_of(i * depth, depth), depth)
        return pltpu.make_async_copy(prod_hbm.at[:, :, part], prod_ref.at[:, :, part], sems.at[i])

    for i in range(chunks):
        copy(i).start()
    inverse, along = scales(extra_ref[...], objectives)
    projection = jnp.sum(along * row_ref[...], axis=1, keepdims=True) / total
    scal_ref[0] = jnp.broadcast_to(inverse, scal_ref.shape[1:])
    scal_ref[1] = jnp.broadcast_to(projection, scal_ref.shape[1:])

    @pl.loop(0, chunks)
    def _(i):
        copy(i).wait()

        @pl.loop(0, depth // LANES)
        def _(k):
            part = pl.ds(pl.multiple_of(i * depth + k * LANES, LANES), LANES)
            grad = prod_ref[0, :, part].astype(F32) * share_ref[0, 0]
            for which in range(1, objectives):
                grad += prod_ref[which, :, part].astype(F32) * share_ref[0, which]
            inverse = scal_ref[0]
            unit = resid_ref[:, part].astype(F32) * inverse
            out_ref[:, part] = (inverse * (gain_ref[:, part] * grad - unit * scal_ref[1])).astype(BF)


def backward(total, resid, gain, prods, grad, share):
    tokens, _ = resid.shape
    tail = grad.shape[1] // LANES - 1
    whole = lambda array: pl.BlockSpec(array.shape, lambda i: (0,) * array.ndim)
    return pl.pallas_call(
        functools.partial(backward_kernel, total),
        out_shape=jax.ShapeDtypeStruct(resid.shape, BF),
        grid=(1,),
        in_specs=[
            smem(),
            whole(share),
            whole(resid),
            whole(gain),
            hbm(),
            pl.BlockSpec((tokens, LANES), lambda i: (0, tail)),
        ],
        out_specs=whole(resid),
        scratch_shapes=[
            pltpu.VMEM(prods.shape, BF),
            pltpu.VMEM((2, tokens, LANES), F32),
            pltpu.SemaphoreType.DMA((4,)),
        ],
        compiler_params=params(BIG),
        cost_estimate=cost(2 * prods.size, 2 * prods.size),
        name="backward",
    )(share, share, resid, gain, prods, grad)


def weight_kernel(plan, order_of, depth, place_ref, gain_ref, wide_ref, grad_ref, *rest):
    count = len(plan)
    block_refs = rest[:-6]
    out_hbm, turned_ref, blocks_ref, result_ref, sems, out_sems = rest[-6:]
    tokens, features = block_refs[0].shape
    columns = grad_ref.shape[2]
    total_tokens = tokens * count
    order, inner = order_of(place_ref[0])
    chunks = sems.shape[1]
    width = features // chunks

    def load(k, source, i):
        place = (pl.ds(k * tokens, tokens), pl.ds(i * width, width))
        return pltpu.make_async_copy(block_refs[source].at[:, place[1]], blocks_ref.at[place], sems.at[k, i])

    for i in range(chunks):
        for k, choice in enumerate(plan):
            if len(choice) == 1:
                load(k, choice[0], i).start()
            else:

                @pl.when(inner == 1)
                def _():
                    load(k, choice[0], i).start()

                @pl.when(inner == 0)
                def _():
                    load(k, choice[1], i).start()

    for k in range(count):
        turned_ref[:, k * tokens : (k + 1) * tokens] = grad_ref[order[k], :tokens, :].T
    start = pl.multiple_of(place_ref[0] * columns, columns)
    scale = wide_ref[:, pl.ds(start, columns)] / total_tokens

    def store(i):
        rows = pl.ds(pl.multiple_of(i * depth, depth), depth)
        return pltpu.make_async_copy(result_ref.at[rows, :], out_hbm.at[rows, :], out_sems.at[i])

    for i in range(chunks):
        for k, choice in enumerate(plan):
            load(k, choice[0], i).wait()

        @pl.loop(i * width // depth, (i + 1) * width // depth)
        def _(step):
            part = pl.ds(pl.multiple_of(step * depth, depth), depth)
            value = jnp.dot(turned_ref[...], blocks_ref[:, part], preferred_element_type=F32)
            result_ref[part, :] = (value * gain_ref[:, part]).T * scale
            store(step).start()

    @pl.loop(0, features // depth)
    def _(step):
        store(step).wait()


def weight_grad(place, gain, wide, grads, blocks, plan, order_of):
    tokens, features = blocks[0].shape
    columns = grads.shape[2]
    depth = 512
    count = len(plan)
    return pl.pallas_call(
        functools.partial(weight_kernel, plan, order_of, depth),
        out_shape=jax.ShapeDtypeStruct((features, columns), F32),
        in_specs=[smem()] + [vmem()] * 3 + [hbm()] * len(blocks),
        out_specs=hbm(),
        scratch_shapes=[
            pltpu.VMEM((columns, tokens * count), BF),
            pltpu.VMEM((tokens * count, features), BF),
            pltpu.VMEM((features, columns), F32),
            pltpu.SemaphoreType.DMA((count, 2)),
            pltpu.SemaphoreType.DMA((features // depth,)),
        ],
        compiler_params=params(BIG),
        cost_estimate=cost(2 * tokens * count * features * columns, 8 * features * columns),
        name="weights",
    )(place, gain, wide, grads, *blocks)


def finish_kernel(total_tokens, sum_ref, got_ref, wide_ref, gain_ref, bias_ref):
    sums = (sum_ref[...] + got_ref[...]) / total_tokens
    gain_ref[...] = sums[0:1]
    bias_ref[...] = sums[1:2] * wide_ref[...]


def finish(total_tokens, sums, got, wide):
    return pl.pallas_call(
        functools.partial(finish_kernel, total_tokens),
        out_shape=(jax.ShapeDtypeStruct((1, sums.shape[1]), F32), jax.ShapeDtypeStruct(wide.shape, F32)),
        in_specs=[vmem()] * 3,
        out_specs=(vmem(), vmem()),
        compiler_params=params(4),
        cost_estimate=cost(4 * sums.size, 16 * sums.size),
        name="finish",
    )(sums, got, wide)


def gather_blocks(resid):
    count = lax.axis_size("tok")
    if count == 8:

        def pairs(moves):
            return [(2 * a + s, 2 * b + s) for a, b in moves for s in range(2)]

        def cross(lines):
            return [(2 * a + s, 2 * a + 1 - s) for a in lines for s in range(2)]

        swap, out = pairs([(1, 2), (2, 1)]), pairs([(1, 0), (2, 3)])
        x0 = lax.ppermute(resid, "tok", cross(range(4)))
        z1 = lax.ppermute(resid, "tok", pairs([(0, 1), (1, 0), (2, 3), (3, 2)]))
        m1 = lax.ppermute(resid, "tok", swap)
        m2 = lax.ppermute(z1, "tok", swap)
        x1 = lax.ppermute(z1, "tok", cross(range(4)))
        f1 = lax.ppermute(m1, "tok", out)
        f2 = lax.ppermute(m2, "tok", out)
        x2m = lax.ppermute(m1, "tok", cross((1, 2)))
        x2e = lax.ppermute(f1, "tok", cross((0, 3)))
        x3m = lax.ppermute(m2, "tok", cross((1, 2)))
        x3e = lax.ppermute(f2, "tok", cross((0, 3)))

        def order_of(place):
            line, side = place // 2, place % 2
            low = line < 2
            inner = jnp.where((line == 1) | (line == 2), 1, 0)
            lines = [line, jnp.where(line % 2 == 0, line + 1, line - 1), jnp.where(low, 2, 1), jnp.where(low, 3, 0)]
            return [2 * a + s for a in lines for s in (side, 1 - side)], inner

        blocks = [resid, x0, z1, x1, m1, f1, x2m, x2e, m2, f2, x3m, x3e]
        plan = ((0,), (1,), (2,), (3,), (4, 5), (6, 7), (8, 9), (10, 11))
        return blocks, plan, order_of
    found = {0: resid}
    for flip in range(2, count, 2):
        found[flip] = exchange(resid, "tok", flip)
    for flip in range(0, count, 2):
        found[flip + 1] = exchange(found[flip], "tok", 1)
    plan = tuple((flip,) for flip in range(count))
    return [found[flip] for flip in range(count)], plan, lambda place: ([place ^ flip for flip in range(count)], 0)


def total_over_tok(value):
    count = lax.axis_size("tok")
    flips = [1 << bit for bit in range(1, count.bit_length() - 1)] + [1]
    got = None
    for step, flip in enumerate(flips):
        if step:
            value = value + got
        got = lax.ppermute(value, "tok", [(i, i ^ flip) for i in range(count)])
    return value, got


def fast_device(resid, norm_gain, head_in, head_bias, head_out, targets, label_mask, obj_weight):
    tokens, features = resid.shape
    objectives, hidden = head_out.shape
    columns = objectives * hidden
    peers = lax.axis_size("tok")
    total_features = features * lax.axis_size("tp")
    total_tokens = tokens * peers
    me = lax.axis_index("tp")
    place = lax.axis_index("tok")
    gain = norm_gain[None, :]
    partner = [(i, i ^ 1) for i in range(4)]
    across = [(i, i ^ 2) for i in range(4)]

    blocks, plan, order_of = gather_blocks(resid)
    held = [pltpu.with_memory_space_constraint(one, pltpu.HBM) for one in (resid, gain, head_in)]
    keep, send = forward((me % 2)[None], *held)
    recv = lax.ppermute(send, "tp", partner)
    mine, send = merge((me // 2)[None], keep, recv)
    recv = lax.ppermute(send, "tp", across)
    gram = gram_of(head_in, objectives, hidden)
    part = heads(
        total_features,
        me[None],
        mine,
        recv,
        head_bias[None, :],
        head_out.reshape(1, columns),
        targets.T,
        label_mask.T,
    )
    part1 = lax.ppermute(part, "tp", partner)
    part2 = lax.ppermute(part, "tp", across)
    part3 = lax.ppermute(part2, "tp", partner)
    grad, message, col_sums = spread(me[None], (part, part1, part2, part3), gram, peers)
    grads = lax.all_to_all(message, "tok", 0, 0)
    prods, along = products(resid, head_in, grad, objectives)
    squares = jnp.sum(grads[:, tokens : tokens + 3, :objectives].astype(F32), axis=(0, 1))
    squares = squares[None, :]
    got = lax.ppermute(squares, "tp", partner)
    squares = squares + got
    got = lax.ppermute(squares, "tp", across)
    entries = total_tokens * total_features
    sums, share, wide = balance_of(entries, squares, got, obj_weight[None, :], along, col_sums)
    sums, got = total_over_tok(sums)
    resid_grad = backward(total_features, resid, gain, prods, grad, share)
    head_in_grad = weight_grad(place[None], gain, wide, grads, blocks, plan, order_of)
    gain_grad, head_bias_grad = finish(total_tokens, sums, got, wide)
    return (resid_grad, gain_grad[0], head_in_grad, head_bias_grad[0])


def head_gradient(preact, head_out, targets, label_mask):
    count = preact.shape[0]
    objectives, hidden = head_out.shape
    cube = preact.reshape(count, objectives, hidden)
    squash = jax.nn.sigmoid(cube)
    scores = jnp.sum(cube * squash * head_out[None], axis=2)
    errors = label_mask.astype(jnp.float32) * (scores - targets)
    slopes = squash * (1.0 + cube * (1.0 - squash))
    row_grad = (errors[:, :, None] * head_out[None] * slopes).astype(jnp.bfloat16)
    return row_grad.reshape(count, objectives * hidden)


def general_device(resid, norm_gain, head_in, head_bias, head_out, targets, label_mask, obj_weight):
    tok_rows = resid.shape[0]
    total_features = resid.shape[1] * lax.axis_size("tp")
    objectives, hidden = head_out.shape
    total_tokens = tok_rows * lax.axis_size("tok")
    floated = resid.astype(jnp.float32)
    row_sums = lax.psum(jnp.sum(floated * floated, axis=1), "tp")
    inverse = lax.rsqrt(row_sums[:, None] / total_features + norm_eps)
    unit = floated * inverse
    normed = (unit * norm_gain[None, :]).astype(jnp.bfloat16)
    partial_value = jnp.dot(normed, head_in, preferred_element_type=jnp.float32)
    quarter = lax.psum_scatter(partial_value, "tp", scatter_dimension=0, tiled=True)
    share = quarter.shape[0]
    offset = lax.axis_index("tp") * share
    part_targets = lax.dynamic_slice_in_dim(targets, offset, share, 0)
    part_mask = lax.dynamic_slice_in_dim(label_mask, offset, share, 0)
    part_grad = head_gradient(quarter + head_bias[None, :], head_out, part_targets, part_mask)
    row_grad = lax.all_gather(part_grad, "tp", axis=0, tiled=True)
    grad_float = row_grad.astype(jnp.float32)

    def objective_square(which):
        grad_slice = lax.dynamic_slice_in_dim(row_grad, which * hidden, hidden, 1)
        weight_slice = lax.dynamic_slice_in_dim(head_in, which * hidden, hidden, 1)
        feature_grad = lax.dot_general(
            grad_slice, weight_slice, (((1,), (1,)), ((), ())), preferred_element_type=jnp.float32
        )
        return jnp.sum(feature_grad * feature_grad)

    local_squares = lax.map(objective_square, jnp.arange(objectives))
    squares = lax.psum(local_squares, ("tok", "tp"))
    obj_rms = jnp.sqrt(squares / (total_tokens * total_features) + grad_eps)
    balance = obj_weight.astype(jnp.float32) / denominator / obj_rms
    balance_cols = jnp.repeat(balance, hidden)
    pre_grad = (grad_float * balance_cols[None, :]).astype(jnp.bfloat16)
    norm_grad = lax.dot_general(
        pre_grad, head_in, (((1,), (1,)), ((), ())), preferred_element_type=jnp.float32
    )
    gain_sum, bias_sum = lax.psum(
        (jnp.sum(norm_grad * unit, axis=0), jnp.sum(grad_float, axis=0)), "tok"
    )
    gain_grad = gain_sum / total_tokens
    head_bias_grad = bias_sum * balance_cols / total_tokens
    projection = lax.psum(jnp.sum(unit * norm_gain[None, :] * norm_grad, axis=1), "tp")
    resid_grad = (
        inverse * (norm_gain[None, :] * norm_grad - unit * (projection[:, None] / total_features))
    ).astype(jnp.bfloat16)
    weight_term = lax.dot_general(
        normed, row_grad, (((0,), (0,)), ((), ())), preferred_element_type=jnp.float32
    )
    summed_block = lax.psum_scatter(weight_term, "tok", scatter_dimension=1, tiled=True)
    columns = summed_block.shape[1]
    col_scale = lax.dynamic_slice_in_dim(balance_cols, lax.axis_index("tok") * columns, columns, 0)
    head_in_grad = summed_block * col_scale[None, :] / total_tokens
    return (resid_grad, gain_grad, head_in_grad, head_bias_grad)


def fits_fast(mesh, resid, head_in, head_out):
    peers, shards = mesh.shape["tok"], mesh.shape["tp"]
    columns = head_in.shape[1]
    tokens, features = resid.shape[0] // peers, resid.shape[1] // shards
    width = columns // peers
    fits = shards == 4 and peers & (peers - 1) == 0 and columns % peers == 0
    fits = fits and peers > 1 and width % LANES == 0 and head_out.shape[1] == LANES and head_out.shape[0] <= 32
    return fits and tokens % 128 == 0 and features % 512 == 0 and columns % 1024 == 0


def solution(mesh):
    def mapped(body):
        return jax.shard_map(
            body,
            mesh=mesh,
            in_specs=(
                P("tok", "tp"),
                P("tp"),
                P("tp", None),
                P(),
                P(),
                P("tok", None),
                P("tok", None),
                P(),
            ),
            out_specs=(P("tok", "tp"), P("tp"), P("tp", "tok"), P()),
            check_vma=False,
        )


    def step(*args):
        if fits_fast(mesh, args[0], args[2], args[4]):
            return mapped(fast_device)(*args)
        return mapped(general_device)(*args)

    return step
```

```python
import functools

import jax
import jax.numpy as jnp
from jax import lax
from jax.experimental import pallas as pl
from jax.experimental.pallas import tpu as pltpu
from jax.sharding import PartitionSpec as P


norm_eps = 1e-05
grad_eps = 1e-06
denominator = 8.0
LANES = 128
BF = jnp.bfloat16
F32 = jnp.float32
MIB = 1 << 20
BIG = 50


def exchange(value, axis, flip):
    count = lax.axis_size(axis)
    return lax.ppermute(value, axis, [(i, i ^ flip) for i in range(count)])


def params(mib):
    return pltpu.CompilerParams(vmem_limit_bytes=mib * MIB)


def cost(flops, nbytes):
    return pl.CostEstimate(flops=int(flops), bytes_accessed=int(nbytes), transcendentals=0)


def vmem():
    return pl.BlockSpec(memory_space=pltpu.VMEM)


def fetch_columns(source, target, sems):
    width = target.shape[1] // sems.shape[0]

    def copy(i):
        part = pl.ds(pl.multiple_of(i * width, width), width)
        return pltpu.make_async_copy(source.at[:, part], target.at[:, part], sems.at[i])

    for i in range(sems.shape[0]):
        copy(i).start()
    return copy, width


def fetch_rows(source, target, sems):
    depth = target.shape[0] // sems.shape[0]

    def copy(i):
        part = pl.ds(pl.multiple_of(i * depth, depth), depth)
        return pltpu.make_async_copy(source.at[part, :], target.at[part, :], sems.at[i])

    for i in range(sems.shape[0]):
        copy(i).start()
    return copy, depth


def smem():
    return pl.BlockSpec(memory_space=pltpu.SMEM)


def hbm():
    return pl.BlockSpec(memory_space=pltpu.HBM)


def forward_kernel(
    core_ref, resid_hbm, gain_hbm, weight_hbm, keep_ref, send_ref, weight_ref, resid_ref, gain_ref, scaled_ref, sems, own_sems
):
    halves, rows, total = keep_ref.shape
    columns = total - LANES
    core = core_ref[0]
    own = [
        pltpu.make_async_copy(resid_hbm, resid_ref, own_sems.at[0]),
        pltpu.make_async_copy(gain_hbm, gain_ref, own_sems.at[1]),
    ]
    for one in own:
        one.start()
    copy, width = fetch_columns(weight_hbm, weight_ref, sems)

    def put(value, cols):
        for quarter in range(2 * halves):
            piece = value[quarter * rows : (quarter + 1) * rows]
            half = quarter // 2

            @pl.when(core == quarter % 2)
            def _():
                keep_ref[half, :, cols] = piece

            @pl.when(core != quarter % 2)
            def _():
                send_ref[half, :, cols] = piece

    for one in own:
        one.wait()
    floated = resid_ref[...].astype(F32)
    scaled_ref[...] = (floated * gain_ref[...]).astype(BF)
    sums = jnp.sum(floated * floated, axis=1, keepdims=True)
    put(jnp.broadcast_to(sums, (sums.shape[0], LANES)), pl.ds(columns, LANES))

    @pl.loop(0, sems.shape[0])
    def _(i):
        copy(i).wait()
        cols = pl.ds(pl.multiple_of(i * width, width), width)
        put(jnp.dot(scaled_ref[...], weight_ref[:, cols], preferred_element_type=F32), cols)


def forward(core, resid, gain, weight):
    tokens, features = resid.shape
    columns = weight.shape[1]
    out = jax.ShapeDtypeStruct((2, tokens // 4, columns + LANES), F32)
    return pl.pallas_call(
        forward_kernel,
        out_shape=(out, out),
        in_specs=[smem(), hbm(), hbm(), hbm()],
        out_specs=(vmem(), vmem()),
        scratch_shapes=[
            pltpu.VMEM(weight.shape, BF),
            pltpu.VMEM((tokens, features), BF),
            pltpu.VMEM((1, features), F32),
            pltpu.VMEM((tokens, features), BF),
            pltpu.SemaphoreType.DMA((4,)),
            pltpu.SemaphoreType.DMA((2,)),
        ],
        compiler_params=params(BIG),
        cost_estimate=cost(2 * tokens * features * columns, 2 * features * columns),
        name="forward",
    )(core, resid, gain, weight)


def merge_kernel(side_ref, keep_ref, recv_ref, mine_ref, send_ref):
    side = side_ref[0]
    mine_ref[...] = keep_ref[side] + recv_ref[side]
    other = keep_ref[1 - side] + recv_ref[1 - side]
    columns = other.shape[1] - LANES
    send_ref[:, :columns] = other[:, :columns].astype(BF)
    tail = other[:, columns:]
    lane = lax.broadcasted_iota(jnp.int32, tail.shape, 1)
    high = tail.astype(BF).astype(F32)
    rest = tail - high
    middle = rest.astype(BF).astype(F32)
    send_ref[:, columns:] = jnp.where(lane == 0, high, jnp.where(lane == 1, middle, rest - middle)).astype(BF)


def merge(side, keep, recv):
    shape = keep.shape[1:]
    return pl.pallas_call(
        merge_kernel,
        out_shape=(jax.ShapeDtypeStruct(shape, F32), jax.ShapeDtypeStruct(shape, BF)),
        in_specs=[pl.BlockSpec(memory_space=pltpu.SMEM), vmem(), vmem()],
        out_specs=(vmem(), vmem()),
        compiler_params=params(8),
        cost_estimate=cost(keep.size, 3 * keep.size),
        name="merge",
    )(side, keep, recv)


def heads_kernel(
    features, me_ref, mine_ref, recv_ref, bias_ref, out_ref, targets_ref, mask_ref, msg_ref, turned_ref
):
    rows = mine_ref.shape[0]
    columns = mine_ref.shape[1] - LANES
    objectives = targets_ref.shape[0]
    hidden = columns // objectives
    start = pl.multiple_of(me_ref[0] * rows, rows)
    turned_ref[0] = targets_ref[...].T
    turned_ref[1] = mask_ref[...].astype(F32).T
    target = turned_ref[0, pl.ds(start, rows), :]
    mask = turned_ref[1, pl.ds(start, rows), :]
    tail = recv_ref[:, columns:].astype(F32)
    sums = mine_ref[:, columns : columns + 1] + ((tail[:, 0:1] + tail[:, 1:2]) + tail[:, 2:3])
    inverse = lax.rsqrt(sums / features + norm_eps)
    lane = lax.broadcasted_iota(jnp.int32, (rows, LANES), 1)
    extra = jnp.zeros((rows, LANES), F32)
    for which in range(objectives):
        cols = slice(which * hidden, (which + 1) * hidden)
        product = (mine_ref[:, cols] + recv_ref[:, cols].astype(F32)) * inverse
        value = product + bias_ref[:, cols]
        squash = jax.nn.sigmoid(value)
        weight = out_ref[:, cols]
        score = jnp.sum(value * squash * weight, axis=1, keepdims=True)
        error = mask[:, which : which + 1] * (score - target[:, which : which + 1])
        grad = (error * weight * (squash * (1.0 + value * (1.0 - squash)))).astype(BF)
        msg_ref[:, cols] = grad
        along = jnp.sum(grad.astype(F32) * product, axis=1, keepdims=True)
        high = along.astype(BF).astype(F32)
        extra = jnp.where(lane == which, high, extra)
        extra = jnp.where(lane == objectives + which, along - high, extra)
    high = inverse.astype(BF).astype(F32)
    rest = inverse - high
    middle = rest.astype(BF).astype(F32)
    extra = jnp.where(lane == 2 * objectives, high, extra)
    extra = jnp.where(lane == 2 * objectives + 1, middle, extra)
    extra = jnp.where(lane == 2 * objectives + 2, rest - middle, extra)
    msg_ref[:, columns:] = extra.astype(BF)


def heads(features, me, mine, recv, bias, head_out, targets, mask):
    tokens = targets.shape[1]
    return pl.pallas_call(
        functools.partial(heads_kernel, features),
        out_shape=jax.ShapeDtypeStruct(mine.shape, BF),
        in_specs=[pl.BlockSpec(memory_space=pltpu.SMEM)] + [vmem()] * 6,
        out_specs=vmem(),
        scratch_shapes=[pltpu.VMEM((2, tokens, targets.shape[0]), F32)],
        compiler_params=params(8),
        cost_estimate=cost(30 * mine.size, 8 * mine.size),
        name="heads",
    )(me, mine, recv, bias, head_out, targets, mask)


def scales(extra, objectives):
    extra = extra.astype(F32)
    at = 2 * objectives
    inverse = (extra[:, at : at + 1] + extra[:, at + 1 : at + 2]) + extra[:, at + 2 : at + 3]
    along = extra[:, :objectives] + extra[:, objectives:at]
    return inverse, along


def gram_kernel(weight_hbm, gram_ref, weight_ref, sems):
    objectives, hidden, _ = gram_ref.shape
    copy, width = fetch_columns(weight_hbm, weight_ref, sems)
    for which in range(objectives):
        if which * hidden % width == 0:
            copy(which * hidden // width).wait()
        block = weight_ref[:, which * hidden : (which + 1) * hidden]
        gram_ref[which] = lax.dot_general(block, block, (((0,), (0,)), ((), ())), preferred_element_type=F32)


def gram_of(weight, objectives, hidden):
    features, columns = weight.shape
    return pl.pallas_call(
        gram_kernel,
        out_shape=jax.ShapeDtypeStruct((objectives, hidden, hidden), F32),
        in_specs=[hbm()],
        out_specs=vmem(),
        scratch_shapes=[pltpu.VMEM(weight.shape, BF), pltpu.SemaphoreType.DMA((4,))],
        compiler_params=params(BIG),
        cost_estimate=cost(2 * features * columns * hidden, 2 * features * columns),
        name="gram",
    )(weight)


def spread_kernel(spot_ref, part0_ref, part1_ref, part2_ref, part3_ref, gram_ref, grad_ref, msg_ref, sums_ref):
    objectives, hidden, _ = gram_ref.shape
    peers, rows, width = msg_ref.shape
    tokens = grad_ref.shape[0]
    columns = objectives * hidden
    share = tokens // 4
    half = tokens // 2
    for flip, part_ref in enumerate((part0_ref, part1_ref, part2_ref, part3_ref)):
        start = pl.multiple_of((spot_ref[0] ^ flip) * share, share)
        grad_ref[pl.ds(start, share), :] = part_ref[...]
    lane = lax.broadcasted_iota(jnp.int32, (1, width), 1)
    squares = jnp.zeros((1, width), F32)
    for which in range(objectives):
        block = grad_ref[:, which * hidden : (which + 1) * hidden]
        pair = lax.dot_general(block, block, (((0,), (0,)), ((), ())), preferred_element_type=F32)
        total = jnp.sum(jnp.sum(pair * gram_ref[which], axis=0, keepdims=True), axis=1, keepdims=True)
        squares = jnp.where(lane == which, total, squares)
    for peer in range(peers):
        piece = grad_ref[:, peer * width : (peer + 1) * width].astype(F32)
        sums_ref[:, peer * width : (peer + 1) * width] = jnp.sum(piece, axis=0, keepdims=True)
    mine = pl.ds(pl.multiple_of(lax.rem(spot_ref[0], 2) * half, half), half)
    inverse, _ = scales(grad_ref[mine, columns:], objectives)
    for peer in range(peers):
        piece = grad_ref[mine, peer * width : (peer + 1) * width].astype(F32)
        msg_ref[peer, :half, :] = (piece * inverse).astype(BF)
    high = squares.astype(BF).astype(F32)
    rest = squares - high
    middle = rest.astype(BF).astype(F32)
    row = lax.broadcasted_iota(jnp.int32, (rows - half, width), 0)
    tail = jnp.where(row == 0, high, jnp.where(row == 1, middle, jnp.where(row == 2, rest - middle, 0.0)))
    for peer in range(peers):
        msg_ref[peer, half:, :] = tail.astype(BF)


def spread(me, parts, gram, peers):
    share, total = parts[0].shape
    tokens = 4 * share
    columns = gram.shape[0] * gram.shape[1]
    return pl.pallas_call(
        spread_kernel,
        out_shape=(
            jax.ShapeDtypeStruct((tokens, total), BF),
            jax.ShapeDtypeStruct((peers, tokens // 2 + 16, columns // peers), BF),
            jax.ShapeDtypeStruct((1, columns), F32),
        ),
        in_specs=[pl.BlockSpec(memory_space=pltpu.SMEM)] + [vmem()] * 5,
        out_specs=(vmem(), vmem(), vmem()),
        compiler_params=params(16),
        cost_estimate=cost(2 * tokens * columns * gram.shape[1], 8 * tokens * total),
        name="spread",
    )(me, *parts, gram)


def products_kernel(resid_ref, weight_hbm, grad_ref, prod_hbm, along_ref, weight_ref, prod_ref, scal_ref, sems, out_sems):
    objectives = along_ref.shape[0]
    columns = weight_hbm.shape[1]
    hidden = columns // objectives
    copy, depth = fetch_rows(weight_hbm, weight_ref, sems)
    inverse, _ = scales(grad_ref[:, columns:], objectives)
    scal_ref[...] = jnp.broadcast_to(inverse, scal_ref.shape)

    def store(i):
        rows = pl.ds(pl.multiple_of(i * depth, depth), depth)
        return pltpu.make_async_copy(prod_ref.at[:, :, rows], prod_hbm.at[:, :, rows], out_sems.at[i])

    @pl.loop(0, sems.shape[0])
    def _(i):
        copy(i).wait()
        rows = pl.ds(pl.multiple_of(i * depth, depth), depth)
        unit = resid_ref[:, rows].astype(F32) * scal_ref[:, 0:1]
        for which in range(objectives):
            cols = slice(which * hidden, (which + 1) * hidden)
            value = lax.dot_general(
                grad_ref[:, cols], weight_ref[rows, cols], (((1,), (1,)), ((), ())), preferred_element_type=F32
            )
            along_ref[which : which + 1, rows] = jnp.sum(value * unit, axis=0, keepdims=True)
            prod_ref[which, :, rows] = value.astype(BF)
        store(i).start()

    @pl.loop(0, sems.shape[0])
    def _(i):
        store(i).wait()


def products(resid, weight, grad, objectives):
    tokens, features = resid.shape
    shape = (objectives, tokens, features)
    return pl.pallas_call(
        products_kernel,
        out_shape=(jax.ShapeDtypeStruct(shape, BF), jax.ShapeDtypeStruct((objectives, features), F32)),
        in_specs=[vmem(), hbm(), vmem()],
        out_specs=(hbm(), vmem()),
        scratch_shapes=[
            pltpu.VMEM(weight.shape, BF),
            pltpu.VMEM(shape, BF),
            pltpu.VMEM((tokens, LANES), F32),
            pltpu.SemaphoreType.DMA((4,)),
            pltpu.SemaphoreType.DMA((4,)),
        ],
        compiler_params=params(BIG),
        cost_estimate=cost(2 * weight.size * tokens, 4 * weight.size),
        name="products",
    )(resid, weight, grad)


def balance_kernel(entries, squares_ref, got_ref, level_ref, along_ref, cols_ref, sums_ref, share_ref, wide_ref):
    objectives = along_ref.shape[0]
    hidden = wide_ref.shape[1] // objectives
    rms = jnp.sqrt((squares_ref[...] + got_ref[...]) / entries + grad_eps)
    share = level_ref[...].astype(F32) / denominator / rms
    share_ref[...] = share
    row = lax.broadcasted_iota(jnp.int32, (objectives, objectives), 0)
    lane = lax.broadcasted_iota(jnp.int32, (objectives, objectives), 1)
    down = jnp.sum(jnp.where(row == lane, share, 0.0), axis=1, keepdims=True)
    sums_ref[0:1, :] = jnp.sum(along_ref[...] * down, axis=0, keepdims=True)
    sums_ref[1:2, :] = cols_ref[...]
    for which in range(objectives):
        wide_ref[:, which * hidden : (which + 1) * hidden] = jnp.broadcast_to(share[:, which : which + 1], (1, hidden))


def balance_of(entries, squares, got, level, along, col_sums):
    objectives, features = along.shape
    columns = col_sums.shape[1]
    return pl.pallas_call(
        functools.partial(balance_kernel, entries),
        out_shape=(
            jax.ShapeDtypeStruct((2, features), F32),
            jax.ShapeDtypeStruct((1, objectives), F32),
            jax.ShapeDtypeStruct((1, columns), F32),
        ),
        in_specs=[vmem()] * 5,
        out_specs=(vmem(), vmem(), vmem()),
        compiler_params=params(4),
        cost_estimate=cost(4 * along.size, 8 * along.size),
        name="balance",
    )(squares, got, level, along, col_sums)


def backward_kernel(total, share_ref, row_ref, resid_ref, gain_ref, prod_hbm, extra_ref, out_ref, prod_ref, scal_ref, sems):
    objectives, _, features = prod_hbm.shape
    chunks = sems.shape[0]
    depth = features // chunks

    def copy(i):
        part = pl.ds(pl.multiple_of(i * depth, depth), depth)
        return pltpu.make_async_copy(prod_hbm.at[:, :, part], prod_ref.at[:, :, part], sems.at[i])

    for i in range(chunks):
        copy(i).start()
    inverse, along = scales(extra_ref[...], objectives)
    projection = jnp.sum(along * row_ref[...], axis=1, keepdims=True) / total
    scal_ref[0] = jnp.broadcast_to(inverse, scal_ref.shape[1:])
    scal_ref[1] = jnp.broadcast_to(projection, scal_ref.shape[1:])

    @pl.loop(0, chunks)
    def _(i):
        copy(i).wait()

        @pl.loop(0, depth // LANES)
        def _(k):
            part = pl.ds(pl.multiple_of(i * depth + k * LANES, LANES), LANES)
            grad = prod_ref[0, :, part].astype(F32) * share_ref[0, 0]
            for which in range(1, objectives):
                grad += prod_ref[which, :, part].astype(F32) * share_ref[0, which]
            inverse = scal_ref[0]
            unit = resid_ref[:, part].astype(F32) * inverse
            out_ref[:, part] = (inverse * (gain_ref[:, part] * grad - unit * scal_ref[1])).astype(BF)


def backward(total, resid, gain, prods, grad, share):
    tokens, _ = resid.shape
    tail = grad.shape[1] // LANES - 1
    whole = lambda array: pl.BlockSpec(array.shape, lambda i: (0,) * array.ndim)
    return pl.pallas_call(
        functools.partial(backward_kernel, total),
        out_shape=jax.ShapeDtypeStruct(resid.shape, BF),
        grid=(1,),
        in_specs=[
            smem(),
            whole(share),
            whole(resid),
            whole(gain),
            hbm(),
            pl.BlockSpec((tokens, LANES), lambda i: (0, tail)),
        ],
        out_specs=whole(resid),
        scratch_shapes=[
            pltpu.VMEM(prods.shape, BF),
            pltpu.VMEM((2, tokens, LANES), F32),
            pltpu.SemaphoreType.DMA((4,)),
        ],
        compiler_params=params(BIG),
        cost_estimate=cost(2 * prods.size, 2 * prods.size),
        name="backward",
    )(share, share, resid, gain, prods, grad)


def weight_kernel(plan, order_of, depth, place_ref, core_ref, gain_ref, wide_ref, grad_ref, other_ref, *rest):
    count = len(plan)
    block_refs = rest[:-7]
    out_hbm, rows_ref, turned_ref, blocks_ref, result_ref, sems, out_sems = rest[-7:]
    tokens, features = block_refs[0].shape
    columns = grad_ref.shape[2]
    total_tokens = tokens * count
    order, inner = order_of(place_ref[0])
    chunks = sems.shape[1]
    width = features // chunks

    def load(k, source, i):
        place = (pl.ds(k * tokens, tokens), pl.ds(i * width, width))
        return pltpu.make_async_copy(block_refs[source].at[:, place[1]], blocks_ref.at[place], sems.at[k, i])

    for i in range(chunks):
        for k, choice in enumerate(plan):
            if len(choice) == 1:
                load(k, choice[0], i).start()
            else:

                @pl.when(inner == 1)
                def _():
                    load(k, choice[0], i).start()

                @pl.when(inner == 0)
                def _():
                    load(k, choice[1], i).start()

    half = tokens // 2
    mine = pl.ds(pl.multiple_of(core_ref[0] * half, half), half)
    theirs = pl.ds(pl.multiple_of((1 - core_ref[0]) * half, half), half)
    for k in range(count):
        rows_ref[k, mine, :] = grad_ref[order[k], :half, :]
        rows_ref[k, theirs, :] = other_ref[order[k], :half, :]
        turned_ref[:, k * tokens : (k + 1) * tokens] = rows_ref[k].T
    start = pl.multiple_of(place_ref[0] * columns, columns)
    scale = wide_ref[:, pl.ds(start, columns)] / total_tokens

    def store(i):
        rows = pl.ds(pl.multiple_of(i * depth, depth), depth)
        return pltpu.make_async_copy(result_ref.at[rows, :], out_hbm.at[rows, :], out_sems.at[i])

    for i in range(chunks):
        for k, choice in enumerate(plan):
            load(k, choice[0], i).wait()

        @pl.loop(i * width // depth, (i + 1) * width // depth)
        def _(step):
            part = pl.ds(pl.multiple_of(step * depth, depth), depth)
            value = jnp.dot(turned_ref[...], blocks_ref[:, part], preferred_element_type=F32)
            result_ref[part, :] = (value * gain_ref[:, part]).T * scale
            store(step).start()

    @pl.loop(0, features // depth)
    def _(step):
        store(step).wait()


def weight_grad(place, core, gain, wide, grads, others, blocks, plan, order_of):
    tokens, features = blocks[0].shape
    columns = grads.shape[2]
    depth = 512
    count = len(plan)
    return pl.pallas_call(
        functools.partial(weight_kernel, plan, order_of, depth),
        out_shape=jax.ShapeDtypeStruct((features, columns), F32),
        in_specs=[smem(), smem()] + [vmem()] * 4 + [hbm()] * len(blocks),
        out_specs=hbm(),
        scratch_shapes=[
            pltpu.VMEM((count, tokens, columns), BF),
            pltpu.VMEM((columns, tokens * count), BF),
            pltpu.VMEM((tokens * count, features), BF),
            pltpu.VMEM((features, columns), F32),
            pltpu.SemaphoreType.DMA((count, 2)),
            pltpu.SemaphoreType.DMA((features // depth,)),
        ],
        compiler_params=params(BIG),
        cost_estimate=cost(2 * tokens * count * features * columns, 8 * features * columns),
        name="weights",
    )(place, core, gain, wide, grads, others, *blocks)


def finish_kernel(total_tokens, sum_ref, got_ref, wide_ref, gain_ref, bias_ref):
    sums = (sum_ref[...] + got_ref[...]) / total_tokens
    gain_ref[...] = sums[0:1]
    bias_ref[...] = sums[1:2] * wide_ref[...]


def finish(total_tokens, sums, got, wide):
    return pl.pallas_call(
        functools.partial(finish_kernel, total_tokens),
        out_shape=(jax.ShapeDtypeStruct((1, sums.shape[1]), F32), jax.ShapeDtypeStruct(wide.shape, F32)),
        in_specs=[vmem()] * 3,
        out_specs=(vmem(), vmem()),
        compiler_params=params(4),
        cost_estimate=cost(4 * sums.size, 16 * sums.size),
        name="finish",
    )(sums, got, wide)


def gather_blocks(resid):
    count = lax.axis_size("tok")
    if count == 8:

        def pairs(moves):
            return [(2 * a + s, 2 * b + s) for a, b in moves for s in range(2)]

        def cross(lines):
            return [(2 * a + s, 2 * a + 1 - s) for a in lines for s in range(2)]

        swap, out = pairs([(1, 2), (2, 1)]), pairs([(1, 0), (2, 3)])
        x0 = lax.ppermute(resid, "tok", cross(range(4)))
        z1 = lax.ppermute(resid, "tok", pairs([(0, 1), (1, 0), (2, 3), (3, 2)]))
        m1 = lax.ppermute(resid, "tok", swap)
        m2 = lax.ppermute(z1, "tok", swap)
        x1 = lax.ppermute(z1, "tok", cross(range(4)))
        f1 = lax.ppermute(m1, "tok", out)
        f2 = lax.ppermute(m2, "tok", out)
        x2m = lax.ppermute(m1, "tok", cross((1, 2)))
        x2e = lax.ppermute(f1, "tok", cross((0, 3)))
        x3m = lax.ppermute(m2, "tok", cross((1, 2)))
        x3e = lax.ppermute(f2, "tok", cross((0, 3)))

        def order_of(place):
            line, side = place // 2, place % 2
            low = line < 2
            inner = jnp.where((line == 1) | (line == 2), 1, 0)
            lines = [line, jnp.where(line % 2 == 0, line + 1, line - 1), jnp.where(low, 2, 1), jnp.where(low, 3, 0)]
            return [2 * a + s for a in lines for s in (side, 1 - side)], inner

        blocks = [resid, x0, z1, x1, m1, f1, x2m, x2e, m2, f2, x3m, x3e]
        plan = ((0,), (1,), (2,), (3,), (4, 5), (6, 7), (8, 9), (10, 11))
        return blocks, plan, order_of
    found = {0: resid}
    for flip in range(2, count, 2):
        found[flip] = exchange(resid, "tok", flip)
    for flip in range(0, count, 2):
        found[flip + 1] = exchange(found[flip], "tok", 1)
    plan = tuple((flip,) for flip in range(count))
    return [found[flip] for flip in range(count)], plan, lambda place: ([place ^ flip for flip in range(count)], 0)


def total_over_tok(value):
    count = lax.axis_size("tok")
    flips = [1 << bit for bit in range(1, count.bit_length() - 1)] + [1]
    got = None
    for step, flip in enumerate(flips):
        if step:
            value = value + got
        got = lax.ppermute(value, "tok", [(i, i ^ flip) for i in range(count)])
    return value, got


def fast_device(resid, norm_gain, head_in, head_bias, head_out, targets, label_mask, obj_weight):
    tokens, features = resid.shape
    objectives, hidden = head_out.shape
    columns = objectives * hidden
    peers = lax.axis_size("tok")
    total_features = features * lax.axis_size("tp")
    total_tokens = tokens * peers
    me = lax.axis_index("tp")
    place = lax.axis_index("tok")
    gain = norm_gain[None, :]
    partner = [(i, i ^ 1) for i in range(4)]
    across = [(i, i ^ 2) for i in range(4)]

    blocks, plan, order_of = gather_blocks(resid)
    held = [pltpu.with_memory_space_constraint(one, pltpu.HBM) for one in (resid, gain, head_in)]
    keep, send = forward((me % 2)[None], *held)
    recv = lax.ppermute(send, "tp", partner)
    mine, send = merge((me // 2)[None], keep, recv)
    recv = lax.ppermute(send, "tp", across)
    gram = gram_of(head_in, objectives, hidden)
    part = heads(
        total_features,
        me[None],
        mine,
        recv,
        head_bias[None, :],
        head_out.reshape(1, columns),
        targets.T,
        label_mask.T,
    )
    part1 = lax.ppermute(part, "tp", partner)
    part2 = lax.ppermute(part, "tp", across)
    part3 = lax.ppermute(part2, "tp", partner)
    grad, message, col_sums = spread(me[None], (part, part1, part2, part3), gram, peers)
    grads = lax.all_to_all(message, "tok", 0, 0)
    prods, along = products(resid, head_in, grad, objectives)
    half = tokens // 2
    squares = jnp.sum(grads[:, half : half + 3, :objectives].astype(F32), axis=(0, 1))
    squares = squares[None, :]
    got = lax.ppermute(squares, "tp", partner)
    squares = squares + got
    got = lax.ppermute(squares, "tp", across)
    others = lax.ppermute(grads, "tp", partner)
    entries = total_tokens * total_features
    sums, share, wide = balance_of(entries, squares, got, obj_weight[None, :], along, col_sums)
    sums, got = total_over_tok(sums)
    resid_grad = backward(total_features, resid, gain, prods, grad, share)
    head_in_grad = weight_grad(place[None], (me % 2)[None], gain, wide, grads, others, blocks, plan, order_of)
    gain_grad, head_bias_grad = finish(total_tokens, sums, got, wide)
    return (resid_grad, gain_grad[0], head_in_grad, head_bias_grad[0])


def head_gradient(preact, head_out, targets, label_mask):
    count = preact.shape[0]
    objectives, hidden = head_out.shape
    cube = preact.reshape(count, objectives, hidden)
    squash = jax.nn.sigmoid(cube)
    scores = jnp.sum(cube * squash * head_out[None], axis=2)
    errors = label_mask.astype(jnp.float32) * (scores - targets)
    slopes = squash * (1.0 + cube * (1.0 - squash))
    row_grad = (errors[:, :, None] * head_out[None] * slopes).astype(jnp.bfloat16)
    return row_grad.reshape(count, objectives * hidden)


def general_device(resid, norm_gain, head_in, head_bias, head_out, targets, label_mask, obj_weight):
    tok_rows = resid.shape[0]
    total_features = resid.shape[1] * lax.axis_size("tp")
    objectives, hidden = head_out.shape
    total_tokens = tok_rows * lax.axis_size("tok")
    floated = resid.astype(jnp.float32)
    row_sums = lax.psum(jnp.sum(floated * floated, axis=1), "tp")
    inverse = lax.rsqrt(row_sums[:, None] / total_features + norm_eps)
    unit = floated * inverse
    normed = (unit * norm_gain[None, :]).astype(jnp.bfloat16)
    partial_value = jnp.dot(normed, head_in, preferred_element_type=jnp.float32)
    quarter = lax.psum_scatter(partial_value, "tp", scatter_dimension=0, tiled=True)
    share = quarter.shape[0]
    offset = lax.axis_index("tp") * share
    part_targets = lax.dynamic_slice_in_dim(targets, offset, share, 0)
    part_mask = lax.dynamic_slice_in_dim(label_mask, offset, share, 0)
    part_grad = head_gradient(quarter + head_bias[None, :], head_out, part_targets, part_mask)
    row_grad = lax.all_gather(part_grad, "tp", axis=0, tiled=True)
    grad_float = row_grad.astype(jnp.float32)

    def objective_square(which):
        grad_slice = lax.dynamic_slice_in_dim(row_grad, which * hidden, hidden, 1)
        weight_slice = lax.dynamic_slice_in_dim(head_in, which * hidden, hidden, 1)
        feature_grad = lax.dot_general(
            grad_slice, weight_slice, (((1,), (1,)), ((), ())), preferred_element_type=jnp.float32
        )
        return jnp.sum(feature_grad * feature_grad)

    local_squares = lax.map(objective_square, jnp.arange(objectives))
    squares = lax.psum(local_squares, ("tok", "tp"))
    obj_rms = jnp.sqrt(squares / (total_tokens * total_features) + grad_eps)
    balance = obj_weight.astype(jnp.float32) / denominator / obj_rms
    balance_cols = jnp.repeat(balance, hidden)
    pre_grad = (grad_float * balance_cols[None, :]).astype(jnp.bfloat16)
    norm_grad = lax.dot_general(
        pre_grad, head_in, (((1,), (1,)), ((), ())), preferred_element_type=jnp.float32
    )
    gain_sum, bias_sum = lax.psum(
        (jnp.sum(norm_grad * unit, axis=0), jnp.sum(grad_float, axis=0)), "tok"
    )
    gain_grad = gain_sum / total_tokens
    head_bias_grad = bias_sum * balance_cols / total_tokens
    projection = lax.psum(jnp.sum(unit * norm_gain[None, :] * norm_grad, axis=1), "tp")
    resid_grad = (
        inverse * (norm_gain[None, :] * norm_grad - unit * (projection[:, None] / total_features))
    ).astype(jnp.bfloat16)
    weight_term = lax.dot_general(
        normed, row_grad, (((0,), (0,)), ((), ())), preferred_element_type=jnp.float32
    )
    summed_block = lax.psum_scatter(weight_term, "tok", scatter_dimension=1, tiled=True)
    columns = summed_block.shape[1]
    col_scale = lax.dynamic_slice_in_dim(balance_cols, lax.axis_index("tok") * columns, columns, 0)
    head_in_grad = summed_block * col_scale[None, :] / total_tokens
    return (resid_grad, gain_grad, head_in_grad, head_bias_grad)


def fits_fast(mesh, resid, head_in, head_out):
    peers, shards = mesh.shape["tok"], mesh.shape["tp"]
    columns = head_in.shape[1]
    tokens, features = resid.shape[0] // peers, resid.shape[1] // shards
    width = columns // peers
    fits = shards == 4 and peers & (peers - 1) == 0 and columns % peers == 0
    fits = fits and peers > 1 and width % LANES == 0 and head_out.shape[1] == LANES and head_out.shape[0] <= 32
    return fits and tokens % 128 == 0 and features % 512 == 0 and columns % 1024 == 0


def solution(mesh):
    def mapped(body):
        return jax.shard_map(
            body,
            mesh=mesh,
            in_specs=(
                P("tok", "tp"),
                P("tp"),
                P("tp", None),
                P(),
                P(),
                P("tok", None),
                P("tok", None),
                P(),
            ),
            out_specs=(P("tok", "tp"), P("tp"), P("tp", "tok"), P()),
            check_vma=False,
        )


    def step(*args):
        if fits_fast(mesh, args[0], args[2], args[4]):
            return mapped(fast_device)(*args)
        return mapped(general_device)(*args)

    return step
```

```python
import functools

import jax
import jax.numpy as jnp
from jax import lax
from jax.experimental import pallas as pl
from jax.experimental.pallas import tpu as pltpu
from jax.sharding import PartitionSpec as P


norm_eps = 1e-05
grad_eps = 1e-06
denominator = 8.0
LANES = 128
BF = jnp.bfloat16
F32 = jnp.float32
MIB = 1 << 20
BIG = 50


def exchange(value, axis, flip):
    count = lax.axis_size(axis)
    return lax.ppermute(value, axis, [(i, i ^ flip) for i in range(count)])


def params(mib):
    return pltpu.CompilerParams(vmem_limit_bytes=mib * MIB)


def cost(flops, nbytes):
    return pl.CostEstimate(flops=int(flops), bytes_accessed=int(nbytes), transcendentals=0)


def vmem():
    return pl.BlockSpec(memory_space=pltpu.VMEM)


def fetch_columns(source, target, sems):
    width = target.shape[1] // sems.shape[0]

    def copy(i):
        part = pl.ds(pl.multiple_of(i * width, width), width)
        return pltpu.make_async_copy(source.at[:, part], target.at[:, part], sems.at[i])

    for i in range(sems.shape[0]):
        copy(i).start()
    return copy, width


def fetch_rows(source, target, sems):
    depth = target.shape[0] // sems.shape[0]

    def copy(i):
        part = pl.ds(pl.multiple_of(i * depth, depth), depth)
        return pltpu.make_async_copy(source.at[part, :], target.at[part, :], sems.at[i])

    for i in range(sems.shape[0]):
        copy(i).start()
    return copy, depth


def smem():
    return pl.BlockSpec(memory_space=pltpu.SMEM)


def hbm():
    return pl.BlockSpec(memory_space=pltpu.HBM)


def forward_kernel(
    core_ref, resid_hbm, gain_hbm, weight_hbm, keep_ref, send_ref, weight_ref, resid_ref, gain_ref, scaled_ref, sems, own_sems
):
    halves, rows, total = keep_ref.shape
    columns = total - LANES
    core = core_ref[0]
    own = [
        pltpu.make_async_copy(resid_hbm, resid_ref, own_sems.at[0]),
        pltpu.make_async_copy(gain_hbm, gain_ref, own_sems.at[1]),
    ]
    for one in own:
        one.start()
    copy, width = fetch_columns(weight_hbm, weight_ref, sems)

    def put(value, cols):
        for quarter in range(2 * halves):
            piece = value[quarter * rows : (quarter + 1) * rows]
            half = quarter // 2

            @pl.when(core == quarter % 2)
            def _():
                keep_ref[half, :, cols] = piece

            @pl.when(core != quarter % 2)
            def _():
                send_ref[half, :, cols] = piece

    for one in own:
        one.wait()
    floated = resid_ref[...].astype(F32)
    scaled_ref[...] = (floated * gain_ref[...]).astype(BF)
    sums = jnp.sum(floated * floated, axis=1, keepdims=True)
    put(jnp.broadcast_to(sums, (sums.shape[0], LANES)), pl.ds(columns, LANES))

    @pl.loop(0, sems.shape[0])
    def _(i):
        copy(i).wait()
        cols = pl.ds(pl.multiple_of(i * width, width), width)
        put(jnp.dot(scaled_ref[...], weight_ref[:, cols], preferred_element_type=F32), cols)


def forward(core, resid, gain, weight):
    tokens, features = resid.shape
    columns = weight.shape[1]
    out = jax.ShapeDtypeStruct((2, tokens // 4, columns + LANES), F32)
    return pl.pallas_call(
        forward_kernel,
        out_shape=(out, out),
        in_specs=[smem(), hbm(), hbm(), hbm()],
        out_specs=(vmem(), vmem()),
        scratch_shapes=[
            pltpu.VMEM(weight.shape, BF),
            pltpu.VMEM((tokens, features), BF),
            pltpu.VMEM((1, features), F32),
            pltpu.VMEM((tokens, features), BF),
            pltpu.SemaphoreType.DMA((4,)),
            pltpu.SemaphoreType.DMA((2,)),
        ],
        compiler_params=params(BIG),
        cost_estimate=cost(2 * tokens * features * columns, 2 * features * columns),
        name="forward",
    )(core, resid, gain, weight)


def merge_kernel(side_ref, keep_ref, recv_ref, mine_ref, send_ref):
    side = side_ref[0]
    mine_ref[...] = keep_ref[side] + recv_ref[side]
    other = keep_ref[1 - side] + recv_ref[1 - side]
    columns = other.shape[1] - LANES
    send_ref[:, :columns] = other[:, :columns].astype(BF)
    tail = other[:, columns:]
    lane = lax.broadcasted_iota(jnp.int32, tail.shape, 1)
    high = tail.astype(BF).astype(F32)
    rest = tail - high
    middle = rest.astype(BF).astype(F32)
    send_ref[:, columns:] = jnp.where(lane == 0, high, jnp.where(lane == 1, middle, rest - middle)).astype(BF)


def merge(side, keep, recv):
    shape = keep.shape[1:]
    return pl.pallas_call(
        merge_kernel,
        out_shape=(jax.ShapeDtypeStruct(shape, F32), jax.ShapeDtypeStruct(shape, BF)),
        in_specs=[pl.BlockSpec(memory_space=pltpu.SMEM), vmem(), vmem()],
        out_specs=(vmem(), vmem()),
        compiler_params=params(8),
        cost_estimate=cost(keep.size, 3 * keep.size),
        name="merge",
    )(side, keep, recv)


def heads_kernel(
    features, me_ref, mine_ref, recv_ref, bias_ref, out_ref, targets_ref, mask_ref, msg_ref, turned_ref, hold_ref
):
    rows = mine_ref.shape[0]
    columns = mine_ref.shape[1] - LANES
    objectives = targets_ref.shape[0]
    hidden = columns // objectives
    start = pl.multiple_of(me_ref[0] * rows, rows)
    turned_ref[0] = targets_ref[...].T
    turned_ref[1] = mask_ref[...].astype(F32).T
    target = turned_ref[0, pl.ds(start, rows), :]
    mask = turned_ref[1, pl.ds(start, rows), :]
    tail = recv_ref[:, columns:].astype(F32)
    sums = mine_ref[:, columns : columns + 1] + ((tail[:, 0:1] + tail[:, 1:2]) + tail[:, 2:3])
    inverse = lax.rsqrt(sums / features + norm_eps)
    spot = lax.broadcasted_iota(jnp.int32, (rows, objectives), 1)
    scores = jnp.zeros((rows, objectives), F32)
    for which in range(objectives):
        cols = slice(which * hidden, (which + 1) * hidden)
        product = (mine_ref[:, cols] + recv_ref[:, cols].astype(F32)) * inverse
        value = product + bias_ref[:, cols]
        squash = jax.nn.sigmoid(value)
        hold_ref[0, :, cols] = product
        hold_ref[1, :, cols] = squash * (1.0 + value * (1.0 - squash))
        score = jnp.sum(value * squash * out_ref[:, cols], axis=1, keepdims=True)
        scores = jnp.where(spot == which, score, scores)
    errors = mask * (scores - target)
    lane = lax.broadcasted_iota(jnp.int32, (rows, LANES), 1)
    alongs = jnp.zeros((rows, LANES), F32)
    for which in range(objectives):
        cols = slice(which * hidden, (which + 1) * hidden)
        grad = (errors[:, which : which + 1] * out_ref[:, cols] * hold_ref[1, :, cols]).astype(BF)
        msg_ref[:, cols] = grad
        along = jnp.sum(grad.astype(F32) * hold_ref[0, :, cols], axis=1, keepdims=True)
        alongs = jnp.where((lane == which) | (lane == objectives + which), along, alongs)
    high = alongs.astype(BF).astype(F32)
    extra = jnp.where(lane < objectives, high, alongs - high)
    high = inverse.astype(BF).astype(F32)
    rest = inverse - high
    middle = rest.astype(BF).astype(F32)
    extra = jnp.where(lane == 2 * objectives, high, extra)
    extra = jnp.where(lane == 2 * objectives + 1, middle, extra)
    extra = jnp.where(lane == 2 * objectives + 2, rest - middle, extra)
    msg_ref[:, columns:] = extra.astype(BF)


def heads(features, me, mine, recv, bias, head_out, targets, mask):
    tokens = targets.shape[1]
    return pl.pallas_call(
        functools.partial(heads_kernel, features),
        out_shape=jax.ShapeDtypeStruct(mine.shape, BF),
        in_specs=[pl.BlockSpec(memory_space=pltpu.SMEM)] + [vmem()] * 6,
        out_specs=vmem(),
        scratch_shapes=[
            pltpu.VMEM((2, tokens, targets.shape[0]), F32),
            pltpu.VMEM((2, mine.shape[0], bias.shape[1]), F32),
        ],
        compiler_params=params(8),
        cost_estimate=cost(30 * mine.size, 8 * mine.size),
        name="heads",
    )(me, mine, recv, bias, head_out, targets, mask)


def scales(extra, objectives):
    extra = extra.astype(F32)
    at = 2 * objectives
    inverse = (extra[:, at : at + 1] + extra[:, at + 1 : at + 2]) + extra[:, at + 2 : at + 3]
    along = extra[:, :objectives] + extra[:, objectives:at]
    return inverse, along


def gram_kernel(weight_hbm, gram_ref, weight_ref, sems):
    objectives, hidden, _ = gram_ref.shape
    copy, width = fetch_columns(weight_hbm, weight_ref, sems)
    for which in range(objectives):
        if which * hidden % width == 0:
            copy(which * hidden // width).wait()
        block = weight_ref[:, which * hidden : (which + 1) * hidden]
        gram_ref[which] = lax.dot_general(block, block, (((0,), (0,)), ((), ())), preferred_element_type=F32)


def gram_of(weight, objectives, hidden):
    features, columns = weight.shape
    return pl.pallas_call(
        gram_kernel,
        out_shape=jax.ShapeDtypeStruct((objectives, hidden, hidden), F32),
        in_specs=[hbm()],
        out_specs=vmem(),
        scratch_shapes=[pltpu.VMEM(weight.shape, BF), pltpu.SemaphoreType.DMA((4,))],
        compiler_params=params(BIG),
        cost_estimate=cost(2 * features * columns * hidden, 2 * features * columns),
        name="gram",
    )(weight)


def spread_kernel(spot_ref, part0_ref, part1_ref, part2_ref, part3_ref, gram_ref, grad_ref, msg_ref, sums_ref):
    objectives, hidden, _ = gram_ref.shape
    peers, rows, width = msg_ref.shape
    tokens = grad_ref.shape[0]
    columns = objectives * hidden
    share = tokens // 4
    half = tokens // 2
    for flip, part_ref in enumerate((part0_ref, part1_ref, part2_ref, part3_ref)):
        start = pl.multiple_of((spot_ref[0] ^ flip) * share, share)
        grad_ref[pl.ds(start, share), :] = part_ref[...]
    lane = lax.broadcasted_iota(jnp.int32, (1, width), 1)
    squares = jnp.zeros((1, width), F32)
    for which in range(objectives):
        block = grad_ref[:, which * hidden : (which + 1) * hidden]
        pair = lax.dot_general(block, block, (((0,), (0,)), ((), ())), preferred_element_type=F32)
        total = jnp.sum(jnp.sum(pair * gram_ref[which], axis=0, keepdims=True), axis=1, keepdims=True)
        squares = jnp.where(lane == which, total, squares)
    for peer in range(peers):
        piece = grad_ref[:, peer * width : (peer + 1) * width].astype(F32)
        sums_ref[:, peer * width : (peer + 1) * width] = jnp.sum(piece, axis=0, keepdims=True)
    mine = pl.ds(pl.multiple_of(lax.rem(spot_ref[0], 2) * half, half), half)
    inverse, _ = scales(grad_ref[mine, columns:], objectives)
    for peer in range(peers):
        piece = grad_ref[mine, peer * width : (peer + 1) * width].astype(F32)
        msg_ref[peer, :half, :] = (piece * inverse).astype(BF)
    high = squares.astype(BF).astype(F32)
    rest = squares - high
    middle = rest.astype(BF).astype(F32)
    row = lax.broadcasted_iota(jnp.int32, (rows - half, width), 0)
    tail = jnp.where(row == 0, high, jnp.where(row == 1, middle, jnp.where(row == 2, rest - middle, 0.0)))
    for peer in range(peers):
        msg_ref[peer, half:, :] = tail.astype(BF)


def spread(me, parts, gram, peers):
    share, total = parts[0].shape
    tokens = 4 * share
    columns = gram.shape[0] * gram.shape[1]
    return pl.pallas_call(
        spread_kernel,
        out_shape=(
            jax.ShapeDtypeStruct((tokens, total), BF),
            jax.ShapeDtypeStruct((peers, tokens // 2 + 16, columns // peers), BF),
            jax.ShapeDtypeStruct((1, columns), F32),
        ),
        in_specs=[pl.BlockSpec(memory_space=pltpu.SMEM)] + [vmem()] * 5,
        out_specs=(vmem(), vmem(), vmem()),
        compiler_params=params(16),
        cost_estimate=cost(2 * tokens * columns * gram.shape[1], 8 * tokens * total),
        name="spread",
    )(me, *parts, gram)


def products_kernel(resid_ref, weight_hbm, grad_ref, prod_hbm, along_ref, weight_ref, prod_ref, scal_ref, sems, out_sems):
    objectives = along_ref.shape[0]
    columns = weight_hbm.shape[1]
    hidden = columns // objectives
    copy, depth = fetch_rows(weight_hbm, weight_ref, sems)
    inverse, _ = scales(grad_ref[:, columns:], objectives)
    scal_ref[...] = jnp.broadcast_to(inverse, scal_ref.shape)

    def store(i):
        rows = pl.ds(pl.multiple_of(i * depth, depth), depth)
        return pltpu.make_async_copy(prod_ref.at[:, :, rows], prod_hbm.at[:, :, rows], out_sems.at[i])

    @pl.loop(0, sems.shape[0])
    def _(i):
        copy(i).wait()
        rows = pl.ds(pl.multiple_of(i * depth, depth), depth)
        unit = resid_ref[:, rows].astype(F32) * scal_ref[:, 0:1]
        for which in range(objectives):
            cols = slice(which * hidden, (which + 1) * hidden)
            value = lax.dot_general(
                grad_ref[:, cols], weight_ref[rows, cols], (((1,), (1,)), ((), ())), preferred_element_type=F32
            )
            along_ref[which : which + 1, rows] = jnp.sum(value * unit, axis=0, keepdims=True)
            prod_ref[which, :, rows] = value.astype(BF)
        store(i).start()

    @pl.loop(0, sems.shape[0])
    def _(i):
        store(i).wait()


def products(resid, weight, grad, objectives):
    tokens, features = resid.shape
    shape = (objectives, tokens, features)
    return pl.pallas_call(
        products_kernel,
        out_shape=(jax.ShapeDtypeStruct(shape, BF), jax.ShapeDtypeStruct((objectives, features), F32)),
        in_specs=[vmem(), hbm(), vmem()],
        out_specs=(hbm(), vmem()),
        scratch_shapes=[
            pltpu.VMEM(weight.shape, BF),
            pltpu.VMEM(shape, BF),
            pltpu.VMEM((tokens, LANES), F32),
            pltpu.SemaphoreType.DMA((4,)),
            pltpu.SemaphoreType.DMA((4,)),
        ],
        compiler_params=params(BIG),
        cost_estimate=cost(2 * weight.size * tokens, 4 * weight.size),
        name="products",
    )(resid, weight, grad)


def balance_kernel(entries, squares_ref, got_ref, level_ref, along_ref, cols_ref, sums_ref, share_ref, wide_ref):
    objectives = along_ref.shape[0]
    hidden = wide_ref.shape[1] // objectives
    rms = jnp.sqrt((squares_ref[...] + got_ref[...]) / entries + grad_eps)
    share = level_ref[...].astype(F32) / denominator / rms
    share_ref[...] = share
    row = lax.broadcasted_iota(jnp.int32, (objectives, objectives), 0)
    lane = lax.broadcasted_iota(jnp.int32, (objectives, objectives), 1)
    down = jnp.sum(jnp.where(row == lane, share, 0.0), axis=1, keepdims=True)
    sums_ref[0:1, :] = jnp.sum(along_ref[...] * down, axis=0, keepdims=True)
    sums_ref[1:2, :] = cols_ref[...]
    for which in range(objectives):
        wide_ref[:, which * hidden : (which + 1) * hidden] = jnp.broadcast_to(share[:, which : which + 1], (1, hidden))


def balance_of(entries, squares, got, level, along, col_sums):
    objectives, features = along.shape
    columns = col_sums.shape[1]
    return pl.pallas_call(
        functools.partial(balance_kernel, entries),
        out_shape=(
            jax.ShapeDtypeStruct((2, features), F32),
            jax.ShapeDtypeStruct((1, objectives), F32),
            jax.ShapeDtypeStruct((1, columns), F32),
        ),
        in_specs=[vmem()] * 5,
        out_specs=(vmem(), vmem(), vmem()),
        compiler_params=params(4),
        cost_estimate=cost(4 * along.size, 8 * along.size),
        name="balance",
    )(squares, got, level, along, col_sums)


def backward_kernel(total, share_ref, row_ref, resid_ref, gain_ref, prod_hbm, extra_ref, out_ref, prod_ref, scal_ref, sems):
    objectives, _, features = prod_hbm.shape
    chunks = sems.shape[0]
    depth = features // chunks

    def copy(i):
        part = pl.ds(pl.multiple_of(i * depth, depth), depth)
        return pltpu.make_async_copy(prod_hbm.at[:, :, part], prod_ref.at[:, :, part], sems.at[i])

    for i in range(chunks):
        copy(i).start()
    inverse, along = scales(extra_ref[...], objectives)
    projection = jnp.sum(along * row_ref[...], axis=1, keepdims=True) / total
    scal_ref[0] = jnp.broadcast_to(inverse, scal_ref.shape[1:])
    scal_ref[1] = jnp.broadcast_to(projection, scal_ref.shape[1:])

    @pl.loop(0, chunks)
    def _(i):
        copy(i).wait()

        @pl.loop(0, depth // LANES)
        def _(k):
            part = pl.ds(pl.multiple_of(i * depth + k * LANES, LANES), LANES)
            grad = prod_ref[0, :, part].astype(F32) * share_ref[0, 0]
            for which in range(1, objectives):
                grad += prod_ref[which, :, part].astype(F32) * share_ref[0, which]
            inverse = scal_ref[0]
            unit = resid_ref[:, part].astype(F32) * inverse
            out_ref[:, part] = (inverse * (gain_ref[:, part] * grad - unit * scal_ref[1])).astype(BF)


def backward(total, resid, gain, prods, grad, share):
    tokens, _ = resid.shape
    tail = grad.shape[1] // LANES - 1
    whole = lambda array: pl.BlockSpec(array.shape, lambda i: (0,) * array.ndim)
    return pl.pallas_call(
        functools.partial(backward_kernel, total),
        out_shape=jax.ShapeDtypeStruct(resid.shape, BF),
        grid=(1,),
        in_specs=[
            smem(),
            whole(share),
            whole(resid),
            whole(gain),
            hbm(),
            pl.BlockSpec((tokens, LANES), lambda i: (0, tail)),
        ],
        out_specs=whole(resid),
        scratch_shapes=[
            pltpu.VMEM(prods.shape, BF),
            pltpu.VMEM((2, tokens, LANES), F32),
            pltpu.SemaphoreType.DMA((8,)),
        ],
        compiler_params=params(BIG),
        cost_estimate=cost(2 * prods.size, 2 * prods.size),
        name="backward",
    )(share, share, resid, gain, prods, grad)


def weight_kernel(plan, order_of, depth, place_ref, core_ref, gain_ref, wide_ref, grad_ref, other_ref, *rest):
    count = len(plan)
    block_refs = rest[:-7]
    out_hbm, rows_ref, turned_ref, blocks_ref, result_ref, sems, out_sems = rest[-7:]
    tokens, features = block_refs[0].shape
    columns = grad_ref.shape[2]
    total_tokens = tokens * count
    order, inner = order_of(place_ref[0])
    chunks = sems.shape[1]
    width = features // chunks

    def load(k, source, i):
        place = (pl.ds(k * tokens, tokens), pl.ds(i * width, width))
        return pltpu.make_async_copy(block_refs[source].at[:, place[1]], blocks_ref.at[place], sems.at[k, i])

    for i in range(chunks):
        for k, choice in enumerate(plan):
            if len(choice) == 1:
                load(k, choice[0], i).start()
            else:

                @pl.when(inner == 1)
                def _():
                    load(k, choice[0], i).start()

                @pl.when(inner == 0)
                def _():
                    load(k, choice[1], i).start()

    half = tokens // 2
    mine = pl.ds(pl.multiple_of(core_ref[0] * half, half), half)
    theirs = pl.ds(pl.multiple_of((1 - core_ref[0]) * half, half), half)
    for k in range(count):
        rows_ref[k, mine, :] = grad_ref[order[k], :half, :]
        rows_ref[k, theirs, :] = other_ref[order[k], :half, :]
        turned_ref[:, k * tokens : (k + 1) * tokens] = rows_ref[k].T
    start = pl.multiple_of(place_ref[0] * columns, columns)
    scale = wide_ref[:, pl.ds(start, columns)] / total_tokens

    def store(i):
        rows = pl.ds(pl.multiple_of(i * depth, depth), depth)
        return pltpu.make_async_copy(result_ref.at[rows, :], out_hbm.at[rows, :], out_sems.at[i])

    for i in range(chunks):
        for k, choice in enumerate(plan):
            load(k, choice[0], i).wait()

        @pl.loop(i * width // depth, (i + 1) * width // depth)
        def _(step):
            part = pl.ds(pl.multiple_of(step * depth, depth), depth)
            value = jnp.dot(turned_ref[...], blocks_ref[:, part], preferred_element_type=F32)
            result_ref[part, :] = (value * gain_ref[:, part]).T * scale
            store(step).start()

    @pl.loop(0, features // depth)
    def _(step):
        store(step).wait()


def weight_grad(place, core, gain, wide, grads, others, blocks, plan, order_of):
    tokens, features = blocks[0].shape
    columns = grads.shape[2]
    depth = 512
    count = len(plan)
    return pl.pallas_call(
        functools.partial(weight_kernel, plan, order_of, depth),
        out_shape=jax.ShapeDtypeStruct((features, columns), F32),
        in_specs=[smem(), smem()] + [vmem()] * 4 + [hbm()] * len(blocks),
        out_specs=hbm(),
        scratch_shapes=[
            pltpu.VMEM((count, tokens, columns), BF),
            pltpu.VMEM((columns, tokens * count), BF),
            pltpu.VMEM((tokens * count, features), BF),
            pltpu.VMEM((features, columns), F32),
            pltpu.SemaphoreType.DMA((count, 2)),
            pltpu.SemaphoreType.DMA((features // depth,)),
        ],
        compiler_params=params(BIG),
        cost_estimate=cost(2 * tokens * count * features * columns, 8 * features * columns),
        name="weights",
    )(place, core, gain, wide, grads, others, *blocks)


def finish_kernel(total_tokens, sum_ref, got_ref, wide_ref, gain_ref, bias_ref):
    sums = (sum_ref[...] + got_ref[...]) / total_tokens
    gain_ref[...] = sums[0:1]
    bias_ref[...] = sums[1:2] * wide_ref[...]


def finish(total_tokens, sums, got, wide):
    return pl.pallas_call(
        functools.partial(finish_kernel, total_tokens),
        out_shape=(jax.ShapeDtypeStruct((1, sums.shape[1]), F32), jax.ShapeDtypeStruct(wide.shape, F32)),
        in_specs=[vmem()] * 3,
        out_specs=(vmem(), vmem()),
        compiler_params=params(4),
        cost_estimate=cost(4 * sums.size, 16 * sums.size),
        name="finish",
    )(sums, got, wide)


def gather_blocks(resid):
    count = lax.axis_size("tok")
    if count == 8:

        def pairs(moves):
            return [(2 * a + s, 2 * b + s) for a, b in moves for s in range(2)]

        def cross(lines):
            return [(2 * a + s, 2 * a + 1 - s) for a in lines for s in range(2)]

        swap, out = pairs([(1, 2), (2, 1)]), pairs([(1, 0), (2, 3)])
        x0 = lax.ppermute(resid, "tok", cross(range(4)))
        z1 = lax.ppermute(resid, "tok", pairs([(0, 1), (1, 0), (2, 3), (3, 2)]))
        m1 = lax.ppermute(resid, "tok", swap)
        m2 = lax.ppermute(z1, "tok", swap)
        x1 = lax.ppermute(z1, "tok", cross(range(4)))
        f1 = lax.ppermute(m1, "tok", out)
        f2 = lax.ppermute(m2, "tok", out)
        x2m = lax.ppermute(m1, "tok", cross((1, 2)))
        x2e = lax.ppermute(f1, "tok", cross((0, 3)))
        x3m = lax.ppermute(m2, "tok", cross((1, 2)))
        x3e = lax.ppermute(f2, "tok", cross((0, 3)))

        def order_of(place):
            line, side = place // 2, place % 2
            low = line < 2
            inner = jnp.where((line == 1) | (line == 2), 1, 0)
            lines = [line, jnp.where(line % 2 == 0, line + 1, line - 1), jnp.where(low, 2, 1), jnp.where(low, 3, 0)]
            return [2 * a + s for a in lines for s in (side, 1 - side)], inner

        blocks = [resid, x0, z1, x1, m1, f1, x2m, x2e, m2, f2, x3m, x3e]
        plan = ((0,), (1,), (2,), (3,), (4, 5), (6, 7), (8, 9), (10, 11))
        return blocks, plan, order_of
    found = {0: resid}
    for flip in range(2, count, 2):
        found[flip] = exchange(resid, "tok", flip)
    for flip in range(0, count, 2):
        found[flip + 1] = exchange(found[flip], "tok", 1)
    plan = tuple((flip,) for flip in range(count))
    return [found[flip] for flip in range(count)], plan, lambda place: ([place ^ flip for flip in range(count)], 0)


def total_over_tok(value):
    count = lax.axis_size("tok")
    flips = [1 << bit for bit in reversed(range(1, count.bit_length() - 1))] + [1]
    got = None
    for step, flip in enumerate(flips):
        if step:
            value = value + got
        got = lax.ppermute(value, "tok", [(i, i ^ flip) for i in range(count)])
    return value, got


def fast_device(resid, norm_gain, head_in, head_bias, head_out, targets, label_mask, obj_weight):
    tokens, features = resid.shape
    objectives, hidden = head_out.shape
    columns = objectives * hidden
    peers = lax.axis_size("tok")
    total_features = features * lax.axis_size("tp")
    total_tokens = tokens * peers
    me = lax.axis_index("tp")
    place = lax.axis_index("tok")
    gain = norm_gain[None, :]
    partner = [(i, i ^ 1) for i in range(4)]
    across = [(i, i ^ 2) for i in range(4)]

    blocks, plan, order_of = gather_blocks(resid)
    held = [pltpu.with_memory_space_constraint(one, pltpu.HBM) for one in (resid, gain, head_in)]
    keep, send = forward((me % 2)[None], *held)
    recv = lax.ppermute(send, "tp", partner)
    mine, send = merge((me // 2)[None], keep, recv)
    recv = lax.ppermute(send, "tp", across)
    gram = gram_of(head_in, objectives, hidden)
    part = heads(
        total_features,
        me[None],
        mine,
        recv,
        head_bias[None, :],
        head_out.reshape(1, columns),
        targets.T,
        label_mask.T,
    )
    part1 = lax.ppermute(part, "tp", partner)
    part2 = lax.ppermute(part, "tp", across)
    part3 = lax.ppermute(part2, "tp", partner)
    grad, message, col_sums = spread(me[None], (part, part1, part2, part3), gram, peers)
    grads = lax.all_to_all(message, "tok", 0, 0)
    prods, along = products(resid, head_in, grad, objectives)
    half = tokens // 2
    squares = jnp.sum(grads[:, half : half + 3, :objectives].astype(F32), axis=(0, 1))
    squares = squares[None, :]
    got = lax.ppermute(squares, "tp", partner)
    squares = squares + got
    got = lax.ppermute(squares, "tp", across)
    others = lax.ppermute(grads, "tp", partner)
    entries = total_tokens * total_features
    sums, share, wide = balance_of(entries, squares, got, obj_weight[None, :], along, col_sums)
    sums, got = total_over_tok(sums)
    resid_grad = backward(total_features, resid, gain, prods, grad, share)
    head_in_grad = weight_grad(place[None], (me % 2)[None], gain, wide, grads, others, blocks, plan, order_of)
    gain_grad, head_bias_grad = finish(total_tokens, sums, got, wide)
    return (resid_grad, gain_grad[0], head_in_grad, head_bias_grad[0])


def head_gradient(preact, head_out, targets, label_mask):
    count = preact.shape[0]
    objectives, hidden = head_out.shape
    cube = preact.reshape(count, objectives, hidden)
    squash = jax.nn.sigmoid(cube)
    scores = jnp.sum(cube * squash * head_out[None], axis=2)
    errors = label_mask.astype(jnp.float32) * (scores - targets)
    slopes = squash * (1.0 + cube * (1.0 - squash))
    row_grad = (errors[:, :, None] * head_out[None] * slopes).astype(jnp.bfloat16)
    return row_grad.reshape(count, objectives * hidden)


def general_device(resid, norm_gain, head_in, head_bias, head_out, targets, label_mask, obj_weight):
    tok_rows = resid.shape[0]
    total_features = resid.shape[1] * lax.axis_size("tp")
    objectives, hidden = head_out.shape
    total_tokens = tok_rows * lax.axis_size("tok")
    floated = resid.astype(jnp.float32)
    row_sums = lax.psum(jnp.sum(floated * floated, axis=1), "tp")
    inverse = lax.rsqrt(row_sums[:, None] / total_features + norm_eps)
    unit = floated * inverse
    normed = (unit * norm_gain[None, :]).astype(jnp.bfloat16)
    partial_value = jnp.dot(normed, head_in, preferred_element_type=jnp.float32)
    quarter = lax.psum_scatter(partial_value, "tp", scatter_dimension=0, tiled=True)
    share = quarter.shape[0]
    offset = lax.axis_index("tp") * share
    part_targets = lax.dynamic_slice_in_dim(targets, offset, share, 0)
    part_mask = lax.dynamic_slice_in_dim(label_mask, offset, share, 0)
    part_grad = head_gradient(quarter + head_bias[None, :], head_out, part_targets, part_mask)
    row_grad = lax.all_gather(part_grad, "tp", axis=0, tiled=True)
    grad_float = row_grad.astype(jnp.float32)

    def objective_square(which):
        grad_slice = lax.dynamic_slice_in_dim(row_grad, which * hidden, hidden, 1)
        weight_slice = lax.dynamic_slice_in_dim(head_in, which * hidden, hidden, 1)
        feature_grad = lax.dot_general(
            grad_slice, weight_slice, (((1,), (1,)), ((), ())), preferred_element_type=jnp.float32
        )
        return jnp.sum(feature_grad * feature_grad)

    local_squares = lax.map(objective_square, jnp.arange(objectives))
    squares = lax.psum(local_squares, ("tok", "tp"))
    obj_rms = jnp.sqrt(squares / (total_tokens * total_features) + grad_eps)
    balance = obj_weight.astype(jnp.float32) / denominator / obj_rms
    balance_cols = jnp.repeat(balance, hidden)
    pre_grad = (grad_float * balance_cols[None, :]).astype(jnp.bfloat16)
    norm_grad = lax.dot_general(
        pre_grad, head_in, (((1,), (1,)), ((), ())), preferred_element_type=jnp.float32
    )
    gain_sum, bias_sum = lax.psum(
        (jnp.sum(norm_grad * unit, axis=0), jnp.sum(grad_float, axis=0)), "tok"
    )
    gain_grad = gain_sum / total_tokens
    head_bias_grad = bias_sum * balance_cols / total_tokens
    projection = lax.psum(jnp.sum(unit * norm_gain[None, :] * norm_grad, axis=1), "tp")
    resid_grad = (
        inverse * (norm_gain[None, :] * norm_grad - unit * (projection[:, None] / total_features))
    ).astype(jnp.bfloat16)
    weight_term = lax.dot_general(
        normed, row_grad, (((0,), (0,)), ((), ())), preferred_element_type=jnp.float32
    )
    summed_block = lax.psum_scatter(weight_term, "tok", scatter_dimension=1, tiled=True)
    columns = summed_block.shape[1]
    col_scale = lax.dynamic_slice_in_dim(balance_cols, lax.axis_index("tok") * columns, columns, 0)
    head_in_grad = summed_block * col_scale[None, :] / total_tokens
    return (resid_grad, gain_grad, head_in_grad, head_bias_grad)


def fits_fast(mesh, resid, head_in, head_out):
    peers, shards = mesh.shape["tok"], mesh.shape["tp"]
    columns = head_in.shape[1]
    tokens, features = resid.shape[0] // peers, resid.shape[1] // shards
    width = columns // peers
    fits = shards == 4 and peers & (peers - 1) == 0 and columns % peers == 0
    fits = fits and peers > 1 and width % LANES == 0 and head_out.shape[1] == LANES and head_out.shape[0] <= 32
    return fits and tokens % 128 == 0 and features % 512 == 0 and columns % 1024 == 0


def solution(mesh):
    def mapped(body):
        return jax.shard_map(
            body,
            mesh=mesh,
            in_specs=(
                P("tok", "tp"),
                P("tp"),
                P("tp", None),
                P(),
                P(),
                P("tok", None),
                P("tok", None),
                P(),
            ),
            out_specs=(P("tok", "tp"), P("tp"), P("tp", "tok"), P()),
            check_vma=False,
        )


    def step(*args):
        if fits_fast(mesh, args[0], args[2], args[4]):
            return mapped(fast_device)(*args)
        return mapped(general_device)(*args)

    return step
```
